256 devices in a mesh: freq: 16 (over y_lo, x, core), row: 16 (over y_hi, z).
Axes of the slice: x: 4, y: 4 (y_hi: 2, y_lo: 2; y = y_hi * 2 + y_lo), z: 8, core: 2. Of those that a mesh axis runs over, the one named last changes fastest.
Arguments:
- source: bfloat16 [16, 2, 256, 512], P('freq', None, 'row'), may hold values from -6 to 6
- receiver: bfloat16 [16, 2, 256, 512], P('freq', None, 'row'), may hold values from -6 to 6
- filters: bfloat16 [16, 2, 2, 25, 25], P('freq'), may hold values from -0.15625 to 0.15625
- table_index: int32 [2, 256, 512], P(None, 'row'), may hold values from 0 to 1
- lags: int32 [16], replicated, may hold values from 0 to 15, each once
- offset_filters: float32 [16, 9, 9], P('freq'), may hold values from -0.125 to 0.125
Outputs:
- image: float32 [2, 16, 256, 512], P(None, 'freq', 'row')
The draws below stay inside these ranges and needn't reach their ends.
Inputs may be any that keep to these rules, and one draw needn't show every extreme that they name: `lags`: each of 0 .. 15 appears exactly once.
All inputs are finite; a program needn't handle non-finite values.
Results may differ from the reference program's by a relative error of at most 0.0052.
Values may be sent and summed in bfloat16 or wider, within the bound.
No kernel may reach another device: no remote copies, remote signals or barrier semaphores. Data moves between devices by JAX's collectives and lax.ppermute only.
A program may use at most 128 MiB of HBM per device.

```python
import jax
import jax.numpy as jnp
from jax import lax

NY = 512
NV = 2
FILT = 25
NOFF = 16
OFILT = 9
DEPTHS = 2
FREQS = 16
NX = 256


def set_ends(entries, stream_key, least, largest):
    spot = [jax.random.randint(jax.random.fold_in(stream_key, axis), (), 0, length) for axis, length in enumerate(entries.shape)]
    main_axis = entries.shape.index(max(entries.shape))
    neighbour = spot[:main_axis] + [(spot[main_axis] + 1) % entries.shape[main_axis]] + spot[main_axis + 1:]
    return entries.at[tuple(spot)].set(least).at[tuple(neighbour)].set(largest)


def levels(key, dims, cuts, smallest, top_value):
    loudness = 1.0
    for dim, parts in cuts:
        heights = jax.random.uniform(jax.random.fold_in(jax.random.fold_in(key, 6), dim), (parts,), jnp.float32, smallest / len(cuts), top_value / len(cuts))
        loudness = loudness * jnp.repeat(jnp.exp(heights), dims[dim] // parts).reshape((-1,) + (1,) * (len(dims) - 1 - dim))
    return loudness


def bell_draw(stream_key, shape, deviation, reach, pieces=(), kind=jnp.bfloat16):
    values = deviation * jax.random.normal(stream_key, shape, jnp.float32)
    if pieces:
        values = values * levels(stream_key, shape, pieces, -0.22, 0.18)
    return jnp.clip(values, -reach, reach).astype(kind)


def setup_inputs(seed: int = 0) -> dict:
    splits = jax.random.split(jax.random.key(seed), 7)
    source = bell_draw(splits[0], (FREQS, 2, NX, NY), 1.0, 6.0, ((0, 16), (2, 16)))
    receiver = bell_draw(splits[1], (FREQS, 2, NX, NY), 1.0, 6.0, ((0, 16), (2, 16)))
    filters = bell_draw(splits[2], (FREQS, NV, 2, FILT, FILT), (2 * FILT * FILT) ** -0.5, 0.15625, ((0, 16),))
    table_index = set_ends(jax.random.randint(splits[3], (DEPTHS, NX, NY), 0, NV), jax.random.fold_in(splits[3], 1), 0, NV - 1).astype(jnp.int32)
    lags = jax.random.permutation(splits[4], NOFF).astype(jnp.int32)
    offset_filters = bell_draw(splits[5], (NOFF, OFILT, OFILT), (2 * OFILT * OFILT * FREQS) ** -0.5, 0.125, ((0, 16),), jnp.float32)
    return dict(source=source, receiver=receiver, filters=filters, table_index=table_index, lags=lags, offset_filters=offset_filters)


def kernel_of(taps, sign):
    real_part = taps[:, 0].astype(jnp.float32)
    imag_part = taps[:, 1].astype(jnp.float32) * sign
    upper = jnp.stack([real_part, -imag_part], 1)
    lower = jnp.stack([imag_part, real_part], 1)
    kernel = jnp.stack([upper, lower], 1)
    return kernel.reshape((NV * 2, 2, FILT, FILT))


def extrapolate(field, filters, index, sign):
    half = (FILT - 1) // 2
    classes = jnp.arange(NV, dtype=jnp.int32)
    hot = (index[None, :, :] == classes[:, None, None]).astype(jnp.float32)

    def one_freq(pair):
        plane, taps = pair
        out = lax.conv_general_dilated(plane[None].astype(jnp.float32), kernel_of(taps, sign), (1, 1),
                                       ((half, half), (half, half)),
                                       dimension_numbers=("NCHW", "OIHW", "NCHW"),
                                       precision=lax.Precision.HIGHEST)[0]
        out = out.reshape((NV, 2, NX, NY))
        return jnp.sum(out * hot[:, None], axis=0).astype(jnp.bfloat16)

    return lax.map(one_freq, (field, filters))


def correlate(source, receiver, lags):
    shift = NOFF // 2
    down_pad = jnp.pad(source, ((0, 0), (0, 0), (0, 0), (shift, shift)))
    up_pad = jnp.pad(receiver, ((0, 0), (0, 0), (0, 0), (shift, shift)))

    def one_lag(lag):
        offset = lag.astype(jnp.int32) - shift
        down = lax.dynamic_slice_in_dim(down_pad, (shift - offset).astype(jnp.int32), NY, 3)
        up = lax.dynamic_slice_in_dim(up_pad, (shift + offset).astype(jnp.int32), NY, 3)
        return jnp.sum(down.astype(jnp.float32) * up.astype(jnp.float32), axis=(0, 1))

    return lax.map(one_lag, lags)


def reference(source, receiver, filters, table_index, lags, offset_filters):
    ohalf = (OFILT - 1) // 2
    raws = []
    for depth in range(DEPTHS):
        source = extrapolate(source, filters, table_index[depth], 1.0)
        receiver = extrapolate(receiver, filters, table_index[depth], -1.0)
        raws.append(correlate(source, receiver, lags))
    raw = jnp.stack(raws)
    kernel = offset_filters[:, None].astype(jnp.float32)
    return lax.conv_general_dilated(raw, kernel, (1, 1), ((ohalf, ohalf), (ohalf, ohalf)),
                                    dimension_numbers=("NCHW", "OIHW", "NCHW"),
                                    feature_group_count=NOFF,
                                    precision=lax.Precision.HIGHEST)
```

```python
import jax
import jax.numpy as jnp
from jax import lax
from jax.experimental import pallas as pl
from jax.experimental.pallas import tpu as pltpu
from jax.sharding import PartitionSpec as P

NV = 2
FILT = 25
HALF = 12
NOFF = 16
OFILT = 9
OHALF = 4
DEPTHS = 2
ROWS = 16
WIDTH = 512
BLK = 64
NB = 8
LANES = 128
EXT = ROWS + 2 * OHALF
MID = EXT + 2 * HALF
TOP = MID + 2 * HALF
LINES = DEPTHS * EXT
SHARE = LINES // NOFF
F32 = jnp.float32
BF16 = jnp.bfloat16


def lane_ids(shape):
    return lax.broadcasted_iota(jnp.int32, shape, len(shape) - 1)


def block_ids(shape):
    return lax.broadcasted_iota(jnp.int32, shape, len(shape) - 2)


def next_block(x):
    rolled = pltpu.roll(x, NB - 1, x.ndim - 2)
    return jnp.where(block_ids(x.shape) == NB - 1, 0.0, rolled)


def prev_block(x):
    rolled = pltpu.roll(x, 1, x.ndim - 2)
    return jnp.where(block_ids(x.shape) == 0, 0.0, rolled)


def swap_halves(x):
    return pltpu.roll(x, BLK, x.ndim - 1)


def ahead(x, nxt, prv, t):
    if t == 0:
        return x
    j = lane_ids(x.shape) % BLK
    if t > 0:
        return pltpu.roll(jnp.where(j < t, nxt, x), LANES - t, x.ndim - 1)
    return pltpu.roll(jnp.where(j >= BLK + t, prv, x), -t, x.ndim - 1)


def prep_kernel(source, receiver, index, pay, low, high):
    lane = lane_ids((8, LANES))
    planes = (
        (source[0, 0].astype(F32), source[0, 1].astype(F32)),
        (receiver[0, 0].astype(F32), -receiver[0, 1].astype(F32)),
        (index[0].astype(F32), index[1].astype(F32)),
    )
    for p, (one, two) in enumerate(planes):
        for group in range(ROWS // 8):
            rows = slice(8 * group, 8 * group + 8)
            blocks = []
            for g in range(WIDTH // LANES):
                u = one[rows, LANES * g : LANES * g + LANES]
                v = two[rows, LANES * g : LANES * g + LANES]
                blocks.append(jnp.where(lane < BLK, u, swap_halves(v)))
                blocks.append(jnp.where(lane < BLK, swap_halves(u), v))
            turned = jnp.swapaxes(jnp.stack(blocks), 0, 1).astype(BF16)
            pay[rows, 8 * p : 8 * p + 8, :] = turned
            if p < 2:
                subs = slice(8 * p, 8 * p + 8)
                if group == 0:
                    high[0:8, subs, :] = turned
                    low[0:4, subs, :] = turned[4:]
                else:
                    high[8:12, subs, :] = turned[:4]
                    low[4:12, subs, :] = turned


def prep(source, receiver, index):
    return pl.pallas_call(
        prep_kernel,
        out_shape=(
            jax.ShapeDtypeStruct((ROWS, 24, LANES), BF16),
            jax.ShapeDtypeStruct((HALF, 16, LANES), BF16),
            jax.ShapeDtypeStruct((HALF, 16, LANES), BF16),
        ),
        name="prep",
    )(source, receiver, index)


def matrix_kernel(filters, out, base):
    tap = lax.broadcasted_iota(jnp.int32, (FILT, LANES), 0)
    col = lane_ids((FILT, LANES)) % BLK
    perm = ((HALF - tap) % BLK == col).astype(BF16)
    for v in range(NV):
        for part in range(2):
            base[2 * v + part, 0:FILT, :] = jnp.dot(
                filters[0, v, part], perm, preferred_element_type=F32
            )
    lane = lane_ids((BLK, LANES))
    gap = jnp.abs(lax.broadcasted_iota(jnp.int32, (BLK, LANES), 0) - lane % BLK)
    near = gap < BLK // 2

    def one_tap(a, carry):
        for v in range(NV):
            turned = []
            for part in range(2):
                row = base[2 * v + part, pl.ds(a, 1), :]
                full = jnp.broadcast_to(row, (BLK, LANES))
                turned.append(pltpu.roll(full, 0, 1, stride=1, stride_axis=0))
            real, imag = turned
            cols = slice(v * LANES, v * LANES + LANES)
            for c in range(2):
                if c == 0:
                    band = jnp.where(lane < BLK, real, imag)
                else:
                    band = jnp.where(lane < BLK, -imag, real)
                out[a, c * BLK : c * BLK + BLK, cols] = jnp.where(near, band, 0.0).astype(BF16)
                out[a, LANES + c * BLK : LANES + c * BLK + BLK, cols] = jnp.where(
                    near, 0.0, band
                ).astype(BF16)
        return carry

    lax.fori_loop(0, FILT, one_tap, 0)


def filter_matrix(filters):
    return pl.pallas_call(
        matrix_kernel,
        out_shape=jax.ShapeDtypeStruct((FILT, 2 * LANES, 2 * LANES), BF16),
        scratch_shapes=[pltpu.VMEM((2 * NV, 32, LANES), F32)],
        name="matrix",
    )(filters)


CHUNK = 8


def place_rows(buffer, start, rows):
    shape = (rows.shape[0], NB, LANES)
    j = lane_ids(shape) % BLK
    for f in range(2):
        x = rows[:, NB * f : NB * f + NB]
        subs = slice(NB * f, NB * f + NB)
        sides = jnp.where(j < BLK // 2, next_block(x), prev_block(x))
        n = rows.shape[0]
        buffer[start : start + n, subs, 0:LANES] = x.astype(BF16)
        buffer[start : start + n, subs, LANES : 2 * LANES] = sides.astype(BF16)


def filter_rows(buffer, matrix, start):
    acc = None
    for a in range(FILT):
        layer = buffer[start + a : start + a + CHUNK].reshape(CHUNK * 16, 2 * LANES)
        term = jnp.dot(layer, matrix[a], preferred_element_type=F32)
        acc = term if acc is None else acc + term
    return acc.reshape(CHUNK, 16, 2 * LANES)


def pick(acc, mask):
    mask = jnp.concatenate([mask, mask], axis=1)
    return jnp.where(mask == 0.0, acc[:, :, :LANES], acc[:, :, LANES:])


def march_kernel(own, up, down, far_up, far_down, matrix, lines, top, mid):
    here = lax.axis_index("row")
    last = lax.axis_size("row") - 1
    place_rows(top, 0, far_up[...].astype(F32))
    place_rows(top, HALF, up[:, 0:16, :].astype(F32))
    place_rows(top, HALF + ROWS, own[:, 0:16, :].astype(F32))
    place_rows(top, HALF + 2 * ROWS, down[:, 0:16, :].astype(F32))
    place_rows(top, HALF + 3 * ROWS, far_down[...].astype(F32))
    lane = lane_ids((CHUNK, NB, LANES))
    for n in range(MID // CHUNK):
        first = CHUNK * n
        block, inner = divmod(first, ROWS)
        both = (up, own, down)[block][inner : inner + CHUNK, 16:24, :].astype(F32)
        mask = jnp.where(lane < BLK, both, swap_halves(both))
        q = pick(filter_rows(top, matrix, first), mask)
        if block == 0:
            q = jnp.where(here > 0, q, 0.0)
        if block == 2:
            q = jnp.where(here < last, q, 0.0)
        q = q.astype(BF16)
        for i in range(CHUNK):
            line = first + i - HALF
            if 0 <= line < EXT:
                lines[line] = q[i]
        place_rows(mid, first, q.astype(F32))
    for n in range(EXT // CHUNK):
        first = CHUNK * n
        pieces = []
        for i in range(CHUNK):
            block, inner = divmod(first + i + HALF, ROWS)
            pieces.append((up, own, down)[block][inner : inner + 1, 16:24, :].astype(F32))
        both = jnp.concatenate(pieces, axis=0)
        mask = jnp.where(lane < BLK, swap_halves(both), both)
        q = pick(filter_rows(mid, matrix, first), mask)
        for i in range(CHUNK):
            block = (first + i + HALF) // ROWS
            line = q[i]
            if block == 0:
                line = jnp.where(here > 0, line, 0.0)
            if block == 2:
                line = jnp.where(here < last, line, 0.0)
            lines[EXT + first + i] = line.astype(BF16)


def march(own, up, down, far_up, far_down, matrix):
    return pl.pallas_call(
        march_kernel,
        out_shape=jax.ShapeDtypeStruct((LINES, 16, LANES), BF16),
        scratch_shapes=[
            pltpu.VMEM((TOP, 16, 2 * LANES), BF16),
            pltpu.VMEM((MID, 16, 2 * LANES), BF16),
        ],
        name="march",
    )(own, up, down, far_up, far_down, matrix)


def gather_kernel(lags, fields, out, src, rec, rec_next, rec_prev, raw):
    lane = lane_ids((NB, LANES))
    nfreq = fields.shape[0] // SHARE
    for n in range(fields.shape[0]):
        line = fields[n].astype(F32)
        src[n] = line[0:NB]
        r = jnp.where(lane < BLK, line[NB : 2 * NB], -line[NB : 2 * NB])
        rec[n] = r
        flipped = swap_halves(r)
        rec_next[n] = next_block(flipped)
        rec_prev[n] = prev_block(flipped)
    for i in range(NOFF):
        h = i - NOFF // 2
        sums = []
        for m in range(SHARE):
            total = None
            for f in range(nfreq):
                n = f * SHARE + m
                side = rec_next if h > 0 else rec_prev
                term = src[n] * ahead(rec[n], side[n], side[n], 2 * h)
                total = term if total is None else total + term
            total = total + swap_halves(total)
            sums.append(ahead(total, next_block(total), prev_block(total), -h))
        raw[i, 0] = jnp.where(lane < BLK, sums[0], sums[1])
        raw[i, 1] = sums[2]
    for k in range(NOFF):
        out[2 * k : 2 * k + 2] = raw[lags[k]]


def gather_lags(lags, fields):
    n = fields.shape[0]
    return pl.pallas_call(
        gather_kernel,
        out_shape=jax.ShapeDtypeStruct((2 * NOFF, NB, LANES), F32),
        in_specs=[
            pl.BlockSpec(memory_space=pltpu.SMEM),
            pl.BlockSpec(memory_space=pltpu.VMEM),
        ],
        scratch_shapes=[pltpu.VMEM((n, NB, LANES), F32)] * 4
        + [pltpu.VMEM((NOFF, 2, NB, LANES), F32)],
        name="lags",
    )(lags, fields)


def image_kernel(taps, raw, out, rows, nxt, prv):
    lane = lane_ids((NB, LANES))

    def piece(depth, x, high):
        line = depth * EXT + x
        s, m = divmod(line, SHARE)
        got = raw[2 * s + m // 2]
        if m == 2 or (m == 1) == high:
            return got
        return swap_halves(got)

    for x in range(EXT):
        v = jnp.where(lane < BLK, piece(0, x, False), piece(1, x, True))
        rows[x] = v
        flipped = swap_halves(v)
        nxt[x] = next_block(flipped)
        prv[x] = prev_block(flipped)
    for group in range(ROWS // 8):
        accs = [None] * 8
        for b in range(OFILT):
            moved = [
                ahead(rows[8 * group + x], nxt[8 * group + x], prv[8 * group + x], b - OHALF)
                for x in range(8 + 2 * OHALF)
            ]
            for a in range(OFILT):
                w = taps[0, a, b]
                for x in range(8):
                    term = moved[x + a] * w
                    accs[x] = term if accs[x] is None else accs[x] + term
        z = jnp.swapaxes(jnp.stack(accs), 0, 1)
        rows8 = slice(8 * group, 8 * group + 8)
        for g in range(WIDTH // LANES):
            even, odd = z[2 * g], z[2 * g + 1]
            cols = slice(LANES * g, LANES * g + LANES)
            out[0, 0, rows8, cols] = jnp.where(lane < BLK, even, swap_halves(odd))
            out[1, 0, rows8, cols] = jnp.where(lane < BLK, swap_halves(even), odd)


def filter_image(taps, raw):
    return pl.pallas_call(
        image_kernel,
        out_shape=jax.ShapeDtypeStruct((DEPTHS, 1, ROWS, WIDTH), F32),
        in_specs=[
            pl.BlockSpec(memory_space=pltpu.SMEM),
            pl.BlockSpec(memory_space=pltpu.VMEM),
        ],
        scratch_shapes=[pltpu.VMEM((EXT, NB, LANES), F32)] * 3,
        name="image",
    )(taps, raw)


def body(source, receiver, filters, table_index, lags, offset_filters):
    count = lax.axis_size("row")

    def shifted(x, step):
        pairs = [(i, i + step) for i in range(count) if 0 <= i + step < count]
        return lax.ppermute(x, "row", pairs)

    own, low, high = prep(source, receiver, table_index)
    up = shifted(own, 1)
    down = shifted(own, -1)
    far_up = shifted(low, 2)
    far_down = shifted(high, -2)
    matrix = filter_matrix(filters)
    lines = march(own, up, down, far_up, far_down, matrix)
    fields = lax.all_to_all(lines, "freq", 0, 0, tiled=True)
    raw = gather_lags(lags, fields)
    raw = lax.all_to_all(raw, "freq", 0, 0, tiled=True)
    return filter_image(offset_filters, raw)


def solution(mesh):
    in_specs = (
        P("freq", None, "row", None),
        P("freq", None, "row", None),
        P("freq", None, None, None, None),
        P(None, "row", None),
        P(),
        P("freq", None, None),
    )
    out_specs = P(None, "freq", "row", None)
    return jax.shard_map(body, mesh=mesh, in_specs=in_specs, out_specs=out_specs, check_vma=False)
```

```python
import jax
import jax.numpy as jnp
import numpy as np
from jax import lax
from jax.experimental import pallas as pl
from jax.experimental.pallas import tpu as pltpu
from jax.sharding import PartitionSpec as P

NV = 2
FILT = 25
HALF = 12
NOFF = 16
OFILT = 9
OHALF = 4
DEPTHS = 2
ROWS = 16
WIDTH = 512
BLK = 64
NB = 8
LANES = 128
EXT = ROWS + 2 * OHALF
MID = EXT + 2 * HALF
LINES = DEPTHS * EXT
SHARE = LINES // NOFF
F32 = jnp.float32
BF16 = jnp.bfloat16


def lane_ids(shape):
    return lax.broadcasted_iota(jnp.int32, shape, len(shape) - 1)


def block_ids(shape):
    return lax.broadcasted_iota(jnp.int32, shape, len(shape) - 2)


def next_block(x):
    rolled = pltpu.roll(x, NB - 1, x.ndim - 2)
    return jnp.where(block_ids(x.shape) == NB - 1, 0.0, rolled)


def prev_block(x):
    rolled = pltpu.roll(x, 1, x.ndim - 2)
    return jnp.where(block_ids(x.shape) == 0, 0.0, rolled)


def swap_halves(x):
    return pltpu.roll(x, BLK, x.ndim - 1)


def ahead(x, nxt, prv, t):
    if t == 0:
        return x
    j = lane_ids(x.shape) % BLK
    if t > 0:
        return pltpu.roll(jnp.where(j < t, nxt, x), LANES - t, x.ndim - 1)
    return pltpu.roll(jnp.where(j >= BLK + t, prv, x), -t, x.ndim - 1)


def prep_kernel(source, receiver, index, own, south, north):
    lane = lane_ids((8, LANES))
    planes = (
        (source[0, 0].astype(F32), source[0, 1].astype(F32)),
        (receiver[0, 0].astype(F32), -receiver[0, 1].astype(F32)),
        (index[0].astype(F32), index[1].astype(F32)),
    )
    for p, (one, two) in enumerate(planes):
        for group in range(ROWS // 8):
            rows = slice(8 * group, 8 * group + 8)
            blocks = []
            for g in range(WIDTH // LANES):
                u = one[rows, LANES * g : LANES * g + LANES]
                v = two[rows, LANES * g : LANES * g + LANES]
                blocks.append(jnp.where(lane < BLK, u, swap_halves(v)))
                blocks.append(jnp.where(lane < BLK, swap_halves(u), v))
            turned = jnp.swapaxes(jnp.stack(blocks), 0, 1).astype(BF16)
            subs = slice(8 * p, 8 * p + 8)
            own[rows, subs, :] = turned
            if p < 2:
                south[rows, subs, :] = turned
                north[rows, subs, :] = turned
            else:
                dest, base = (north, 0) if group == 0 else (south, 4)
                for i in range(OHALF):
                    dest[ROWS + i // 2, 8 * (i % 2) : 8 * (i % 2) + 8, :] = turned[base + i]


def in_vmem(*arrays):
    return [pltpu.with_memory_space_constraint(x, pltpu.VMEM) for x in arrays]


PARAMS = pltpu.CompilerParams(vmem_limit_bytes=12 << 20)
VSPEC = pl.BlockSpec(memory_space=pltpu.VMEM)
SSPEC = pl.BlockSpec(memory_space=pltpu.SMEM)


def prep(source, receiver, index):
    send = pltpu.VMEM((ROWS + 2, 16, LANES), BF16)
    return pl.pallas_call(
        prep_kernel,
        out_shape=(pltpu.VMEM((ROWS, 24, LANES), BF16), send, send),
        out_specs=(VSPEC, VSPEC, VSPEC),
        compiler_params=PARAMS,
        name="prep",
    )(source, receiver, index)


def matrix_kernel(filters, out, base):
    tap = lax.broadcasted_iota(jnp.int32, (FILT, LANES), 0)
    col = lane_ids((FILT, LANES)) % BLK
    perm = ((HALF - tap) % BLK == col).astype(BF16)
    for v in range(NV):
        for part in range(2):
            base[2 * v + part, 0:FILT, :] = jnp.dot(
                filters[0, v, part], perm, preferred_element_type=F32
            )
    lane = lane_ids((16, LANES))
    row = lax.broadcasted_iota(jnp.int32, (16, LANES), 0)
    zero = jnp.zeros((16, LANES), BF16)

    def one_tap(a):
        for v in range(NV):
            turned = []
            for part in range(2):
                taps = jnp.broadcast_to(base[2 * v + part, pl.ds(a, 1), :], (BLK, LANES))
                turned.append(pltpu.roll(taps, 0, 1, stride=1, stride_axis=0))
            cols = slice(v * LANES, v * LANES + LANES)
            for top in range(0, BLK, 16):
                real, imag = (x[top : top + 16] for x in turned)
                near = jnp.abs(row + top - lane % BLK) < BLK // 2
                for c in range(2):
                    if c == 0:
                        band = jnp.where(lane < BLK, real, imag)
                    else:
                        band = jnp.where(lane < BLK, -imag, real)
                    at = c * BLK + top
                    if top in (0, BLK - 16):
                        out[a, at : at + 16, cols] = jnp.where(near, band, 0.0).astype(BF16)
                        at += LANES
                        out[a, at : at + 16, cols] = jnp.where(near, 0.0, band).astype(BF16)
                    else:
                        out[a, at : at + 16, cols] = band.astype(BF16)
                        at += LANES
                        out[a, at : at + 16, cols] = zero

    for a in range(FILT):
        one_tap(a)


def filter_matrix(filters):
    return pl.pallas_call(
        matrix_kernel,
        out_shape=pltpu.VMEM((FILT, 2 * LANES, 2 * LANES), BF16),
        out_specs=VSPEC,
        scratch_shapes=[pltpu.VMEM((2 * NV, 32, LANES), F32)],
        compiler_params=PARAMS,
        name="matrix",
    )(filters)


def place_rows(buffer, start, rows):
    n = rows.shape[0]
    j = lane_ids((n, NB, LANES)) % BLK
    for f in range(2):
        subs = slice(NB * f, NB * f + NB)
        x = rows[:, subs]
        sides = jnp.where(j < BLK // 2, next_block(x), prev_block(x))
        buffer[start : start + n, subs, 0:LANES] = x.astype(BF16)
        buffer[start : start + n, subs, LANES : 2 * LANES] = sides.astype(BF16)


def filter_rows(buffer, matrix):
    acc = None
    for a in range(FILT):
        layer = buffer[a : a + EXT].reshape(EXT * 16, 2 * LANES)
        term = jnp.dot(layer, matrix[a], preferred_element_type=F32)
        acc = term if acc is None else acc + term
    return acc.reshape(EXT, 16, 2 * LANES)


def pick(acc, own, up, down, depth):
    here = lax.axis_index("row")
    last = lax.axis_size("row") - 1
    lane = lane_ids((NB, LANES))
    rows = []
    for x in range(EXT):
        i = x - OHALF
        if 0 <= i < ROWS:
            both = own[i, 16:24, :].astype(F32)
        else:
            i = x % ROWS
            pack = up if x < OHALF else down
            i = i % OHALF
            both = pack[ROWS + i // 2, 8 * (i % 2) : 8 * (i % 2) + 8, :].astype(F32)
        swapped = swap_halves(both)
        mask = jnp.where(lane < BLK, both, swapped) if depth == 0 else jnp.where(lane < BLK, swapped, both)
        mask = jnp.concatenate([mask, mask], axis=0)
        q = jnp.where(mask == 0.0, acc[x, :, :LANES], acc[x, :, LANES:])
        if x < OHALF:
            q = jnp.where(here > 0, q, 0.0)
        if x >= OHALF + ROWS:
            q = jnp.where(here < last, q, 0.0)
        rows.append(q.astype(BF16))
    return rows


def first_kernel(own, up, down, matrix, lines, south, north, top):
    here = lax.axis_index("row")
    last = lax.axis_size("row") - 1
    place_rows(top, 0, jnp.where(here > 0, up[0:ROWS].astype(F32), 0.0))
    place_rows(top, ROWS, own[:, 0:16, :].astype(F32))
    place_rows(top, 2 * ROWS, jnp.where(here < last, down[0:ROWS].astype(F32), 0.0))
    rows = pick(filter_rows(top, matrix), own, up, down, 0)
    for x, q in enumerate(rows):
        lines[x] = q
        i = x - OHALF
        if 0 <= i < HALF:
            north[i] = q
        if ROWS - HALF <= i < ROWS:
            south[i - OHALF] = q


def first_step(own, up, down, matrix):
    send = pltpu.VMEM((HALF, 16, LANES), BF16)
    return pl.pallas_call(
        first_kernel,
        out_shape=(pltpu.VMEM((EXT, 16, LANES), BF16), send, send),
        in_specs=[VSPEC] * 4,
        out_specs=(VSPEC,) * 3,
        scratch_shapes=[pltpu.VMEM((MID, 16, 2 * LANES), BF16)],
        compiler_params=PARAMS,
        name="first",
    )(*in_vmem(own, up, down, matrix))


def second_kernel(own, up, down, matrix, done, above, below, lines, mid):
    here = lax.axis_index("row")
    last = lax.axis_size("row") - 1
    place_rows(mid, 0, jnp.where(here > 0, above[...].astype(F32), 0.0))
    place_rows(mid, HALF, done[...].astype(F32))
    place_rows(mid, HALF + EXT, jnp.where(here < last, below[...].astype(F32), 0.0))
    lines[0:EXT] = done[...]
    rows = pick(filter_rows(mid, matrix), own, up, down, 1)
    for x, q in enumerate(rows):
        lines[EXT + x] = q


def second_step(own, up, down, matrix, done, above, below):
    return pl.pallas_call(
        second_kernel,
        out_shape=pltpu.VMEM((LINES, 16, LANES), BF16),
        in_specs=[VSPEC] * 7,
        out_specs=VSPEC,
        scratch_shapes=[pltpu.VMEM((MID, 16, 2 * LANES), BF16)],
        compiler_params=PARAMS,
        name="second",
    )(*in_vmem(own, up, down, matrix, done, above, below))


def shift_table():
    k = np.arange(2 * LANES)[:, None]
    n = np.arange(NOFF * LANES)[None, :]
    group, c, j = k // LANES, k % LANES // BLK, k % BLK
    want = n % BLK + 2 * (n // LANES - NOFF // 2)
    same = (n % LANES // BLK == c) & (want % BLK == j)
    inside = (want >= 0) & (want < BLK)
    sign = np.where(c == 0, 1.0, -1.0)
    return (same & (inside == (group == 0))) * sign


def gather_kernel(lags, fields, table, out, src, rec, raw):
    lane = lane_ids((NB, LANES))
    j = lane % BLK
    nfreq = fields.shape[0] // SHARE
    for n in range(fields.shape[0]):
        f, m = divmod(n, SHARE)
        line = fields[n].astype(F32)
        src[m, NB * f : NB * f + NB, :] = line[0:NB]
        r = line[NB : 2 * NB]
        sides = jnp.where(j < BLK // 2, next_block(r), prev_block(r))
        rec[m, NB * f : NB * f + NB, 0:LANES] = r.astype(BF16)
        rec[m, NB * f : NB * f + NB, LANES : 2 * LANES] = sides.astype(BF16)
    for i in range(0, NOFF, 2):
        sums = [[], []]
        for m in range(SHARE):
            moved = jnp.dot(
                rec[m], table[:, LANES * i : LANES * i + 2 * LANES], preferred_element_type=F32
            )
            for e in range(2):
                h = i + e - NOFF // 2
                term = (moved[:, LANES * e : LANES * e + LANES] * src[m]).reshape(nfreq, NB, LANES)
                total = jnp.sum(term, axis=0)
                total = total + swap_halves(total)
                sums[e].append(ahead(total, next_block(total), prev_block(total), -h))
        for e in range(2):
            raw[i + e, 0] = jnp.where(lane < BLK, sums[e][0], sums[e][1])
            raw[i + e, 1] = sums[e][2]
    for k in range(NOFF):
        out[2 * k : 2 * k + 2] = raw[lags[k]]


def gather_lags(lags, fields):
    nfreq = fields.shape[0] // SHARE
    table = jnp.asarray(shift_table(), BF16)
    return pl.pallas_call(
        gather_kernel,
        out_shape=pltpu.VMEM((2 * NOFF, NB, LANES), F32),
        in_specs=[SSPEC, VSPEC, VSPEC],
        out_specs=VSPEC,
        scratch_shapes=[
            pltpu.VMEM((SHARE, NB * nfreq, LANES), F32),
            pltpu.VMEM((SHARE, NB * nfreq, 2 * LANES), BF16),
            pltpu.VMEM((NOFF, 2, NB, LANES), F32),
        ],
        compiler_params=PARAMS,
        name="lags",
    )(lags, *in_vmem(fields, table))


def image_kernel(taps, raw, out, rows, nxt, prv):
    lane = lane_ids((NB, LANES))

    def piece(depth, x, high):
        line = depth * EXT + x
        s, m = divmod(line, SHARE)
        got = raw[2 * s + m // 2]
        if m == 2 or (m == 1) == high:
            return got
        return swap_halves(got)

    for x in range(EXT):
        v = jnp.where(lane < BLK, piece(0, x, False), piece(1, x, True))
        rows[x] = v
        flipped = swap_halves(v)
        nxt[x] = next_block(flipped)
        prv[x] = prev_block(flipped)
    for group in range(ROWS // 8):
        accs = [None] * 8
        for b in range(OFILT):
            moved = [
                ahead(rows[8 * group + x], nxt[8 * group + x], prv[8 * group + x], b - OHALF)
                for x in range(8 + 2 * OHALF)
            ]
            for a in range(OFILT):
                w = taps[0, a, b]
                for x in range(8):
                    term = moved[x + a] * w
                    accs[x] = term if accs[x] is None else accs[x] + term
        z = jnp.swapaxes(jnp.stack(accs), 0, 1)
        rows8 = slice(8 * group, 8 * group + 8)
        for g in range(WIDTH // LANES):
            even, odd = z[2 * g], z[2 * g + 1]
            cols = slice(LANES * g, LANES * g + LANES)
            out[0, 0, rows8, cols] = jnp.where(lane < BLK, even, swap_halves(odd))
            out[1, 0, rows8, cols] = jnp.where(lane < BLK, swap_halves(even), odd)


def filter_image(taps, raw):
    return pl.pallas_call(
        image_kernel,
        out_shape=jax.ShapeDtypeStruct((DEPTHS, 1, ROWS, WIDTH), F32),
        in_specs=[SSPEC, VSPEC],
        scratch_shapes=[pltpu.VMEM((EXT, NB, LANES), F32)] * 3,
        compiler_params=PARAMS,
        name="image",
    )(taps, *in_vmem(raw))


def body(source, receiver, filters, table_index, lags, offset_filters):
    count = lax.axis_size("row")

    def shifted(x, step):
        return lax.ppermute(x, "row", [(i, (i + step) % count) for i in range(count)])

    own, south, north = prep(source, receiver, table_index)
    up = shifted(south, 1)
    down = shifted(north, -1)
    matrix = filter_matrix(filters)
    done, south, north = first_step(own, up, down, matrix)
    above = shifted(north, 1)
    below = shifted(south, -1)
    lines = second_step(own, up, down, matrix, done, above, below)
    fields = lax.all_to_all(lines, "freq", 0, 0, tiled=True)
    raw = gather_lags(lags, fields)
    raw = lax.all_to_all(raw, "freq", 0, 0, tiled=True)
    return filter_image(offset_filters, raw)


def solution(mesh):
    in_specs = (
        P("freq", None, "row", None),
        P("freq", None, "row", None),
        P("freq", None, None, None, None),
        P(None, "row", None),
        P(),
        P("freq", None, None),
    )
    out_specs = P(None, "freq", "row", None)
    return jax.shard_map(body, mesh=mesh, in_specs=in_specs, out_specs=out_specs, check_vma=False)
```

```python
import jax
import jax.numpy as jnp
import numpy as np
from jax import lax
from jax.experimental import pallas as pl
from jax.experimental.pallas import tpu as pltpu
from jax.sharding import PartitionSpec as P

NV = 2
FILT = 25
HALF = 12
NOFF = 16
OFILT = 9
OHALF = 4
DEPTHS = 2
ROWS = 16
WIDTH = 512
BLK = 64
NB = 8
LANES = 128
EXT = ROWS + 2 * OHALF
MID = EXT + 2 * HALF
LINES = DEPTHS * EXT
SHARE = LINES // NOFF
F32 = jnp.float32
BF16 = jnp.bfloat16


def lane_ids(shape):
    return lax.broadcasted_iota(jnp.int32, shape, len(shape) - 1)


def block_ids(shape):
    return lax.broadcasted_iota(jnp.int32, shape, len(shape) - 2)


def next_block(x):
    rolled = pltpu.roll(x, NB - 1, x.ndim - 2)
    return jnp.where(block_ids(x.shape) == NB - 1, 0.0, rolled)


def prev_block(x):
    rolled = pltpu.roll(x, 1, x.ndim - 2)
    return jnp.where(block_ids(x.shape) == 0, 0.0, rolled)


def swap_halves(x):
    return pltpu.roll(x, BLK, x.ndim - 1)


def ahead(x, nxt, prv, t):
    if t == 0:
        return x
    j = lane_ids(x.shape) % BLK
    if t > 0:
        return pltpu.roll(jnp.where(j < t, nxt, x), LANES - t, x.ndim - 1)
    return pltpu.roll(jnp.where(j >= BLK + t, prv, x), -t, x.ndim - 1)


def prep_kernel(source_in, receiver_in, index_in, own, south, north, source, receiver, index, sems):
    copies = [
        pltpu.make_async_copy(one, two, sems.at[i])
        for i, (one, two) in enumerate(
            ((source_in, source), (receiver_in, receiver), (index_in, index))
        )
    ]
    for copy in copies:
        copy.start()
    for copy in copies:
        copy.wait()
    lane = lane_ids((8, LANES))
    planes = (
        (source[0, 0].astype(F32), source[0, 1].astype(F32)),
        (receiver[0, 0].astype(F32), -receiver[0, 1].astype(F32)),
        (index[0].astype(F32), index[1].astype(F32)),
    )
    for p, (one, two) in enumerate(planes):
        classes = []
        for group in range(ROWS // 8):
            rows = slice(8 * group, 8 * group + 8)
            blocks = []
            for g in range(WIDTH // LANES):
                u = one[rows, LANES * g : LANES * g + LANES]
                v = two[rows, LANES * g : LANES * g + LANES]
                blocks.append(jnp.where(lane < BLK, u, swap_halves(v)))
                blocks.append(jnp.where(lane < BLK, swap_halves(u), v))
            turned = jnp.swapaxes(jnp.stack(blocks), 0, 1)
            subs = slice(8 * p, 8 * p + 8)
            own[rows, subs, :] = turned.astype(BF16)
            if p < 2:
                south[rows, subs, :] = turned.astype(BF16)
                north[rows, subs, :] = turned.astype(BF16)
            classes += [turned[i] for i in range(8)]
        if p == 2:
            for i in range(OHALF):
                at = (ROWS + i // 2, slice(8 * (i % 2), 8 * (i % 2) + 8))
                north[at] = classes[i].astype(BF16)
                south[at] = classes[ROWS - OHALF + i].astype(BF16)


def in_vmem(*arrays):
    return [pltpu.with_memory_space_constraint(x, pltpu.VMEM) for x in arrays]


PARAMS = pltpu.CompilerParams(vmem_limit_bytes=12 << 20)
VSPEC = pl.BlockSpec(memory_space=pltpu.VMEM)
SSPEC = pl.BlockSpec(memory_space=pltpu.SMEM)


HBM = pl.BlockSpec(memory_space=pltpu.HBM)


def prep(source, receiver, index):
    send = pltpu.VMEM((ROWS + 2, 16, LANES), BF16)
    return pl.pallas_call(
        prep_kernel,
        out_shape=(pltpu.VMEM((ROWS, 24, LANES), BF16), send, send),
        in_specs=[HBM] * 3,
        out_specs=(VSPEC, VSPEC, VSPEC),
        scratch_shapes=[
            pltpu.VMEM(source.shape, BF16),
            pltpu.VMEM(receiver.shape, BF16),
            pltpu.VMEM(index.shape, jnp.int32),
            pltpu.SemaphoreType.DMA((3,)),
        ],
        compiler_params=PARAMS,
        name="prep",
    )(*[pltpu.with_memory_space_constraint(x, pltpu.HBM) for x in (source, receiver, index)])


def matrix_kernel(filters, taps, out, splats, base):
    tap = lax.broadcasted_iota(jnp.int32, (FILT, LANES), 0)
    col = lane_ids((FILT, LANES)) % BLK
    perm = ((HALF - tap) % BLK == col).astype(BF16)
    for v in range(NV):
        for part in range(2):
            base[2 * v + part, 0:FILT, :] = jnp.dot(
                filters[0, v, part], perm, preferred_element_type=F32
            )
    lane = lane_ids((16, LANES))
    row = lax.broadcasted_iota(jnp.int32, (16, LANES), 0)
    zero = jnp.zeros((16, LANES), BF16)

    def one_tap(a):
        for v in range(NV):
            turned = []
            for part in range(2):
                taps = jnp.broadcast_to(base[2 * v + part, pl.ds(a, 1), :], (BLK, LANES))
                turned.append(pltpu.roll(taps, 0, 1, stride=1, stride_axis=0))
            cols = slice(v * LANES, v * LANES + LANES)
            for top in range(0, BLK, 16):
                real, imag = (x[top : top + 16] for x in turned)
                near = jnp.abs(row + top - lane % BLK) < BLK // 2
                for c in range(2):
                    if c == 0:
                        band = jnp.where(lane < BLK, real, imag)
                    else:
                        band = jnp.where(lane < BLK, -imag, real)
                    at = c * BLK + top
                    if top in (0, BLK - 16):
                        out[a, at : at + 16, cols] = jnp.where(near, band, 0.0).astype(BF16)
                        at += LANES
                        out[a, at : at + 16, cols] = jnp.where(near, 0.0, band).astype(BF16)
                    else:
                        out[a, at : at + 16, cols] = band.astype(BF16)
                        at += LANES
                        out[a, at : at + 16, cols] = zero

    for a in range(FILT):
        one_tap(a)
    for a in range(OFILT):
        for b in range(OFILT):
            splats[OFILT * a + b] = jnp.broadcast_to(taps[a, 0:1, b : b + 1], (NB, LANES))


def filter_matrix(filters, taps):
    return pl.pallas_call(
        matrix_kernel,
        out_shape=(
            pltpu.VMEM((FILT, 2 * LANES, 2 * LANES), BF16),
            pltpu.VMEM((OFILT * OFILT, NB, LANES), F32),
        ),
        out_specs=(VSPEC, VSPEC),
        scratch_shapes=[pltpu.VMEM((2 * NV, 32, LANES), F32)],
        compiler_params=PARAMS,
        name="matrix",
    )(filters, taps)


def place_rows(buffer, start, rows):
    n = rows.shape[0]
    j = lane_ids((n, NB, LANES)) % BLK
    for f in range(2):
        subs = slice(NB * f, NB * f + NB)
        x = rows[:, subs]
        sides = jnp.where(j < BLK // 2, next_block(x), prev_block(x))
        buffer[start : start + n, subs, 0:LANES] = x.astype(BF16)
        buffer[start : start + n, subs, LANES : 2 * LANES] = sides.astype(BF16)


def filter_rows(buffer, matrix):
    acc = None
    for a in range(FILT):
        layer = buffer[a : a + EXT].reshape(EXT * 16, 2 * LANES)
        term = jnp.dot(layer, matrix[a], preferred_element_type=F32)
        acc = term if acc is None else acc + term
    return acc.reshape(EXT, 16, 2 * LANES)


def pick(acc, own, up, down, depth):
    here = lax.axis_index("row")
    last = lax.axis_size("row") - 1
    lane = lane_ids((NB, LANES))
    rows = []
    for x in range(EXT):
        i = x - OHALF
        if 0 <= i < ROWS:
            both = own[i, 16:24, :].astype(F32)
        else:
            pack, i = (up, x) if x < OHALF else (down, i - ROWS)
            both = pack[ROWS + i // 2, 8 * (i % 2) : 8 * (i % 2) + 8, :].astype(F32)
        swapped = swap_halves(both)
        if depth == 0:
            mask = jnp.where(lane < BLK, both, swapped)
        else:
            mask = jnp.where(lane < BLK, swapped, both)
        mask = jnp.concatenate([mask, mask], axis=0)
        both = acc[x // HALF][x % HALF]
        q = jnp.where(mask == 0.0, both[:, :LANES], both[:, LANES:])
        if x < OHALF:
            q = jnp.where(here > 0, q, 0.0)
        if x >= OHALF + ROWS:
            q = jnp.where(here < last, q, 0.0)
        rows.append(q)
    return rows


def place_sides(buffer, up, down, n, middle):
    here = lax.axis_index("row")
    last = lax.axis_size("row") - 1
    place_rows(buffer, 0, jnp.where(here > 0, up[0:n].astype(F32), 0.0))
    place_rows(buffer, n + middle, jnp.where(here < last, down[0:n].astype(F32), 0.0))


def first_kernel(own, up, down, matrix, lines, south, north, top):
    place_rows(top, ROWS, own[:, 0:16, :].astype(F32))
    place_sides(top, up, down, ROWS, ROWS)
    acc = filter_rows(top, matrix)
    rows = pick((acc[0:HALF], acc[HALF:EXT]), own, up, down, 0)
    for x, q in enumerate(rows):
        lines[x] = q.astype(BF16)
    for i in range(HALF):
        south[i] = rows[OHALF + i].astype(BF16)
        north[i] = rows[2 * OHALF + i].astype(BF16)


def first_step(own, up, down, matrix):
    send = pltpu.VMEM((HALF, 16, LANES), BF16)
    return pl.pallas_call(
        first_kernel,
        out_shape=(pltpu.VMEM((EXT, 16, LANES), BF16), send, send),
        in_specs=[VSPEC] * 4,
        out_specs=(VSPEC,) * 3,
        scratch_shapes=[pltpu.VMEM((MID, 16, 2 * LANES), BF16)],
        compiler_params=PARAMS,
        name="first",
    )(*in_vmem(own, up, down, matrix))


def inner_kernel(done, matrix, acc, lines, mid):
    zero = jnp.zeros((HALF, 16, 2 * LANES), BF16)
    mid[0:HALF] = zero
    mid[HALF + EXT :] = zero
    place_rows(mid, HALF, done[...].astype(F32))
    acc[...] = filter_rows(mid, matrix)
    lines[...] = done[...]


def inner_step(done, matrix):
    return pl.pallas_call(
        inner_kernel,
        out_shape=(
            pltpu.VMEM((EXT, 16, 2 * LANES), F32),
            pltpu.VMEM((EXT, 16, LANES), BF16),
        ),
        in_specs=[VSPEC] * 2,
        out_specs=(VSPEC, VSPEC),
        scratch_shapes=[pltpu.VMEM((MID, 16, 2 * LANES), BF16)],
        compiler_params=PARAMS,
        name="inner",
    )(*in_vmem(done, matrix))


def outer_kernel(own, up, down, matrix, part, done, above, below, lines, high, low):
    zero = jnp.zeros((HALF, 16, 2 * LANES), BF16)
    here = lax.axis_index("row")
    last = lax.axis_size("row") - 1
    place_rows(high, 0, jnp.where(here > 0, above[...].astype(F32), 0.0))
    high[HALF:] = zero
    low[0:HALF] = zero
    place_rows(low, HALF, jnp.where(here < last, below[...].astype(F32), 0.0))
    lines[0:EXT] = done[...]

    def edge(buffer, shift, taps):
        acc = None
        for a in taps:
            layer = buffer[a - shift : a - shift + HALF].reshape(HALF * 16, 2 * LANES)
            term = jnp.dot(layer, matrix[a], preferred_element_type=F32)
            acc = term if acc is None else acc + term
        return acc.reshape(HALF, 16, 2 * LANES)

    top = part[0:HALF] + edge(high, 0, range(HALF))
    bottom = part[HALF:EXT] + edge(low, HALF, range(HALF + 1, FILT))
    for x, q in enumerate(pick((top, bottom), own, up, down, 1)):
        lines[EXT + x] = q.astype(BF16)


def outer_step(own, up, down, matrix, part, done, above, below):
    return pl.pallas_call(
        outer_kernel,
        out_shape=pltpu.VMEM((LINES, 16, LANES), BF16),
        in_specs=[VSPEC] * 8,
        out_specs=VSPEC,
        scratch_shapes=[pltpu.VMEM((EXT, 16, 2 * LANES), BF16)] * 2,
        compiler_params=PARAMS,
        name="outer",
    )(*in_vmem(own, up, down, matrix, part, done, above, below))


def shift_table():
    k = np.arange(2 * LANES)[:, None]
    n = np.arange(NOFF * LANES)[None, :]
    group, c, j = k // LANES, k % LANES // BLK, k % BLK
    want = n % BLK + 2 * (n // LANES - NOFF // 2)
    same = (n % LANES // BLK == c) & (want % BLK == j)
    inside = (want >= 0) & (want < BLK)
    sign = np.where(c == 0, 1.0, -1.0)
    return (same & (inside == (group == 0))) * sign


def gather_kernel(lags, fields, table, out, src, rec, raw):
    lane = lane_ids((NB, LANES))
    j = lane % BLK
    nfreq = fields.shape[0] // SHARE
    for n in range(fields.shape[0]):
        f, m = divmod(n, SHARE)
        line = fields[n].astype(F32)
        src[m, NB * f : NB * f + NB, :] = line[0:NB]
        r = line[NB : 2 * NB]
        sides = jnp.where(j < BLK // 2, next_block(r), prev_block(r))
        rec[m, NB * f : NB * f + NB, 0:LANES] = r.astype(BF16)
        rec[m, NB * f : NB * f + NB, LANES : 2 * LANES] = sides.astype(BF16)
    for i in range(0, NOFF, 2):
        sums = [[], []]
        for m in range(SHARE):
            moved = jnp.dot(
                rec[m], table[:, LANES * i : LANES * i + 2 * LANES], preferred_element_type=F32
            )
            for e in range(2):
                h = i + e - NOFF // 2
                term = (moved[:, LANES * e : LANES * e + LANES] * src[m]).reshape(nfreq, NB, LANES)
                total = jnp.sum(term, axis=0)
                total = total + swap_halves(total)
                sums[e].append(ahead(total, next_block(total), prev_block(total), -h))
        for e in range(2):
            raw[i + e, 0] = jnp.where(lane < BLK, sums[e][0], sums[e][1])
            raw[i + e, 1] = sums[e][2]
    for k in range(NOFF):
        out[2 * k : 2 * k + 2] = raw[lags[k]]


def gather_lags(lags, fields):
    nfreq = fields.shape[0] // SHARE
    table = jnp.asarray(shift_table(), BF16)
    return pl.pallas_call(
        gather_kernel,
        out_shape=pltpu.VMEM((2 * NOFF, NB, LANES), F32),
        in_specs=[SSPEC, VSPEC, VSPEC],
        out_specs=VSPEC,
        scratch_shapes=[
            pltpu.VMEM((SHARE, NB * nfreq, LANES), F32),
            pltpu.VMEM((SHARE, NB * nfreq, 2 * LANES), BF16),
            pltpu.VMEM((NOFF, 2, NB, LANES), F32),
        ],
        compiler_params=PARAMS,
        name="lags",
    )(lags, *in_vmem(fields, table))


def image_kernel(splats, raw, out, rows, nxt, prv, image, sems):
    lane = lane_ids((NB, LANES))

    def piece(depth, x, high):
        line = depth * EXT + x
        s, m = divmod(line, SHARE)
        got = raw[2 * s + m // 2]
        if m == 2 or (m == 1) == high:
            return got
        return swap_halves(got)

    for x in range(EXT):
        v = jnp.where(lane < BLK, piece(0, x, False), piece(1, x, True))
        rows[x] = v
        flipped = swap_halves(v)
        nxt[x] = next_block(flipped)
        prv[x] = prev_block(flipped)
    copies = []
    for group in range(ROWS // 8):
        accs = [None] * 8
        for b in range(OFILT):
            moved = [
                ahead(rows[8 * group + x], nxt[8 * group + x], prv[8 * group + x], b - OHALF)
                for x in range(8 + 2 * OHALF)
            ]
            for a in range(OFILT):
                w = splats[OFILT * a + b]
                for x in range(8):
                    term = moved[x + a] * w
                    accs[x] = term if accs[x] is None else accs[x] + term
        z = jnp.swapaxes(jnp.stack(accs), 0, 1)
        for g in range(WIDTH // LANES):
            even, odd = z[2 * g], z[2 * g + 1]
            cols = slice(LANES * g, LANES * g + LANES)
            image[group, 0, 0, :, cols] = jnp.where(lane < BLK, even, swap_halves(odd))
            image[group, 1, 0, :, cols] = jnp.where(lane < BLK, swap_halves(even), odd)

        copy = pltpu.make_async_copy(
            image.at[group], out.at[:, :, pl.ds(8 * group, 8), :], sems.at[group]
        )
        copy.start()
        copies.append(copy)
    for copy in copies:
        copy.wait()


def filter_image(splats, raw):
    return pl.pallas_call(
        image_kernel,
        out_shape=jax.ShapeDtypeStruct((DEPTHS, 1, ROWS, WIDTH), F32),
        in_specs=[VSPEC, VSPEC],
        out_specs=HBM,
        scratch_shapes=[pltpu.VMEM((EXT, NB, LANES), F32)] * 3
        + [
            pltpu.VMEM((ROWS // 8, DEPTHS, 1, 8, WIDTH), F32),
            pltpu.SemaphoreType.DMA((ROWS // 8,)),
        ],
        compiler_params=PARAMS,
        name="image",
    )(*in_vmem(splats, raw))


def body(source, receiver, filters, table_index, lags, offset_filters):
    count = lax.axis_size("row")

    def shifted(x, step):
        return lax.ppermute(x, "row", [(i, (i + step) % count) for i in range(count)])

    own, south, north = prep(source, receiver, table_index)
    up = shifted(south, 1)
    down = shifted(north, -1)
    matrix, splats = filter_matrix(filters, jnp.transpose(offset_filters, (1, 0, 2)))
    done, south, north = first_step(own, up, down, matrix)
    above = shifted(south, 1)
    below = shifted(north, -1)
    part, done = inner_step(done, matrix)
    lines = outer_step(own, up, down, matrix, part, done, above, below)
    fields = lax.all_to_all(lines, "freq", 0, 0, tiled=True)
    raw = gather_lags(lags, fields)
    raw = lax.all_to_all(raw, "freq", 0, 0, tiled=True)
    return filter_image(splats, raw)


def solution(mesh):
    in_specs = (
        P("freq", None, "row", None),
        P("freq", None, "row", None),
        P("freq", None, None, None, None),
        P(None, "row", None),
        P(),
        P("freq", None, None),
    )
    out_specs = P(None, "freq", "row", None)
    return jax.shard_map(body, mesh=mesh, in_specs=in_specs, out_specs=out_specs, check_vma=False)
```

```python
import jax
import jax.numpy as jnp
import numpy as np
from jax import lax
from jax.experimental import pallas as pl
from jax.experimental.pallas import tpu as pltpu
from jax.sharding import PartitionSpec as P

NV = 2
FILT = 25
HALF = 12
NOFF = 16
OFILT = 9
OHALF = 4
DEPTHS = 2
ROWS = 16
WIDTH = 512
BLK = 64
NB = 8
LANES = 128
EXT = ROWS + 2 * OHALF
MID = EXT + 2 * HALF
LINES = DEPTHS * EXT
SHARE = LINES // NOFF
F32 = jnp.float32
BF16 = jnp.bfloat16


def lane_ids(shape):
    return lax.broadcasted_iota(jnp.int32, shape, len(shape) - 1)


def block_ids(shape):
    return lax.broadcasted_iota(jnp.int32, shape, len(shape) - 2)


def next_block(x):
    rolled = pltpu.roll(x, NB - 1, x.ndim - 2)
    return jnp.where(block_ids(x.shape) == NB - 1, 0.0, rolled)


def prev_block(x):
    rolled = pltpu.roll(x, 1, x.ndim - 2)
    return jnp.where(block_ids(x.shape) == 0, 0.0, rolled)


def swap_halves(x):
    return pltpu.roll(x, BLK, x.ndim - 1)


def ahead(x, nxt, prv, t):
    if t == 0:
        return x
    j = lane_ids(x.shape) % BLK
    if t > 0:
        return pltpu.roll(jnp.where(j < t, nxt, x), LANES - t, x.ndim - 1)
    return pltpu.roll(jnp.where(j >= BLK + t, prv, x), -t, x.ndim - 1)


def prep_kernel(
    source_in, receiver_in, index_in, filters_in, taps_in,
    own, south, north, filters, taps,
    source, receiver, index, sems,
):
    copies = [
        pltpu.make_async_copy(one, two, sems.at[i])
        for i, (one, two) in enumerate(
            (
                (source_in, source),
                (receiver_in, receiver),
                (index_in, index),
                (filters_in, filters),
                (taps_in, taps),
            )
        )
    ]
    for copy in copies:
        copy.start()
    for copy in copies:
        copy.wait()
    lane = lane_ids((8, LANES))
    planes = (
        (source[0, 0].astype(F32), source[0, 1].astype(F32)),
        (receiver[0, 0].astype(F32), -receiver[0, 1].astype(F32)),
        (index[0].astype(F32), index[1].astype(F32)),
    )
    for p, (one, two) in enumerate(planes):
        classes = []
        for group in range(ROWS // 8):
            rows = slice(8 * group, 8 * group + 8)
            blocks = []
            for g in range(WIDTH // LANES):
                u = one[rows, LANES * g : LANES * g + LANES]
                v = two[rows, LANES * g : LANES * g + LANES]
                blocks.append(jnp.where(lane < BLK, u, swap_halves(v)))
                blocks.append(jnp.where(lane < BLK, swap_halves(u), v))
            turned = jnp.swapaxes(jnp.stack(blocks), 0, 1)
            subs = slice(8 * p, 8 * p + 8)
            own[rows, subs, :] = turned.astype(BF16)
            if p < 2:
                south[rows, subs, :] = turned.astype(BF16)
                north[rows, subs, :] = turned.astype(BF16)
            classes += [turned[i] for i in range(8)]
        if p == 2:
            for i in range(OHALF):
                at = (ROWS + i // 2, slice(8 * (i % 2), 8 * (i % 2) + 8))
                north[at] = classes[i].astype(BF16)
                south[at] = classes[ROWS - OHALF + i].astype(BF16)


def in_vmem(*arrays):
    return [pltpu.with_memory_space_constraint(x, pltpu.VMEM) for x in arrays]


PARAMS = pltpu.CompilerParams(vmem_limit_bytes=12 << 20)
VSPEC = pl.BlockSpec(memory_space=pltpu.VMEM)
SSPEC = pl.BlockSpec(memory_space=pltpu.SMEM)


HBM = pl.BlockSpec(memory_space=pltpu.HBM)


def prep(*args):
    source, receiver, index, filters, taps = args
    send = pltpu.VMEM((ROWS + 2, 16, LANES), BF16)
    return pl.pallas_call(
        prep_kernel,
        out_shape=(
            pltpu.VMEM((ROWS, 24, LANES), BF16),
            send,
            send,
            pltpu.VMEM(filters.shape, BF16),
            pltpu.VMEM(taps.shape, F32),
        ),
        in_specs=[HBM] * 5,
        out_specs=(VSPEC,) * 5,
        scratch_shapes=[
            pltpu.VMEM(source.shape, BF16),
            pltpu.VMEM(receiver.shape, BF16),
            pltpu.VMEM(index.shape, jnp.int32),
            pltpu.SemaphoreType.DMA((5,)),
        ],
        compiler_params=PARAMS,
        name="prep",
    )(*[pltpu.with_memory_space_constraint(x, pltpu.HBM) for x in args])


def matrix_kernel(filters, taps, out, splats, flat, base):
    tap = lax.broadcasted_iota(jnp.int32, (FILT, LANES), 0)
    col = lane_ids((FILT, LANES)) % BLK
    perm = ((HALF - tap) % BLK == col).astype(BF16)
    for v in range(NV):
        for a in range(FILT):
            flat[v, 2 * a : 2 * a + 2, 0:FILT] = filters[0, v, a].astype(F32)
        base[v] = jnp.dot(
            flat[v, 0 : 2 * FILT, 0:FILT].astype(BF16), perm, preferred_element_type=F32
        )
    lane = lane_ids((16, LANES))
    row = lax.broadcasted_iota(jnp.int32, (16, LANES), 0)
    zero = jnp.zeros((16, LANES), BF16)

    def one_tap(a):
        for v in range(NV):
            turned = []
            for part in range(2):
                taps = jnp.broadcast_to(base[v, 2 * a + part : 2 * a + part + 1, :], (BLK, LANES))
                turned.append(pltpu.roll(taps, 0, 1, stride=1, stride_axis=0))
            cols = slice(v * LANES, v * LANES + LANES)
            for top in range(0, BLK, 16):
                real, imag = (x[top : top + 16] for x in turned)
                near = jnp.abs(row + top - lane % BLK) < BLK // 2
                for c in range(2):
                    if c == 0:
                        band = jnp.where(lane < BLK, real, imag)
                    else:
                        band = jnp.where(lane < BLK, -imag, real)
                    at = c * BLK + top
                    if top in (0, BLK - 16):
                        out[a, at : at + 16, cols] = jnp.where(near, band, 0.0).astype(BF16)
                        at += LANES
                        out[a, at : at + 16, cols] = jnp.where(near, 0.0, band).astype(BF16)
                    else:
                        out[a, at : at + 16, cols] = band.astype(BF16)
                        at += LANES
                        out[a, at : at + 16, cols] = zero

    for a in range(FILT):
        one_tap(a)
    for a in range(OFILT):
        for b in range(OFILT):
            splats[OFILT * a + b] = jnp.broadcast_to(taps[a, 0:1, b : b + 1], (NB, LANES))


def filter_matrix(filters, taps):
    return pl.pallas_call(
        matrix_kernel,
        out_shape=(
            pltpu.VMEM((FILT, 2 * LANES, 2 * LANES), BF16),
            pltpu.VMEM((OFILT * OFILT, NB, LANES), F32),
        ),
        out_specs=(VSPEC, VSPEC),
        scratch_shapes=[
            pltpu.VMEM((NV, 56, LANES), F32),
            pltpu.VMEM((NV, 2 * FILT, LANES), F32),
        ],
        compiler_params=PARAMS,
        name="matrix",
    )(*in_vmem(filters, taps))


def place_rows(buffer, start, rows):
    n = rows.shape[0]
    j = lane_ids((n, NB, LANES)) % BLK
    for f in range(2):
        subs = slice(NB * f, NB * f + NB)
        x = rows[:, subs]
        sides = jnp.where(j < BLK // 2, next_block(x), prev_block(x))
        buffer[start : start + n, subs, 0:LANES] = x.astype(BF16)
        buffer[start : start + n, subs, LANES : 2 * LANES] = sides.astype(BF16)


def filter_rows(buffer, matrix):
    acc = None
    for a in range(FILT):
        layer = buffer[a : a + EXT].reshape(EXT * 16, 2 * LANES)
        term = jnp.dot(layer, matrix[a], preferred_element_type=F32)
        acc = term if acc is None else acc + term
    return acc.reshape(EXT, 16, 2 * LANES)


def pick(acc, own, up, down, depth):
    here = lax.axis_index("row")
    last = lax.axis_size("row") - 1
    lane = lane_ids((NB, LANES))
    rows = []
    for x in range(EXT):
        i = x - OHALF
        if 0 <= i < ROWS:
            both = own[i, 16:24, :].astype(F32)
        else:
            pack, i = (up, x) if x < OHALF else (down, i - ROWS)
            both = pack[ROWS + i // 2, 8 * (i % 2) : 8 * (i % 2) + 8, :].astype(F32)
        swapped = swap_halves(both)
        if depth == 0:
            mask = jnp.where(lane < BLK, both, swapped)
        else:
            mask = jnp.where(lane < BLK, swapped, both)
        mask = jnp.concatenate([mask, mask], axis=0)
        both = acc[x // HALF][x % HALF]
        q = jnp.where(mask == 0.0, both[:, :LANES], both[:, LANES:])
        if x < OHALF:
            q = jnp.where(here > 0, q, 0.0)
        if x >= OHALF + ROWS:
            q = jnp.where(here < last, q, 0.0)
        rows.append(q)
    return rows


def place_sides(buffer, up, down, n, middle):
    here = lax.axis_index("row")
    last = lax.axis_size("row") - 1
    place_rows(buffer, 0, jnp.where(here > 0, up[0:n].astype(F32), 0.0))
    place_rows(buffer, n + middle, jnp.where(here < last, down[0:n].astype(F32), 0.0))


def first_kernel(own, up, down, matrix, lines, south, north, top):
    place_rows(top, ROWS, own[:, 0:16, :].astype(F32))
    place_sides(top, up, down, ROWS, ROWS)
    acc = filter_rows(top, matrix)
    rows = pick((acc[0:HALF], acc[HALF:EXT]), own, up, down, 0)
    for x, q in enumerate(rows):
        lines[x] = q.astype(BF16)
    for i in range(HALF):
        south[i] = rows[OHALF + i].astype(BF16)
        north[i] = rows[2 * OHALF + i].astype(BF16)


def first_step(own, up, down, matrix):
    send = pltpu.VMEM((HALF, 16, LANES), BF16)
    return pl.pallas_call(
        first_kernel,
        out_shape=(pltpu.VMEM((EXT, 16, LANES), BF16), send, send),
        in_specs=[VSPEC] * 4,
        out_specs=(VSPEC,) * 3,
        scratch_shapes=[pltpu.VMEM((MID, 16, 2 * LANES), BF16)],
        compiler_params=PARAMS,
        name="first",
    )(*in_vmem(own, up, down, matrix))


def inner_kernel(done, matrix, acc, lines, mid):
    zero = jnp.zeros((HALF, 16, 2 * LANES), BF16)
    mid[0:HALF] = zero
    mid[HALF + EXT :] = zero
    place_rows(mid, HALF, done[...].astype(F32))
    acc[...] = filter_rows(mid, matrix)
    lines[...] = done[...]


def inner_step(done, matrix):
    return pl.pallas_call(
        inner_kernel,
        out_shape=(
            pltpu.VMEM((EXT, 16, 2 * LANES), F32),
            pltpu.VMEM((EXT, 16, LANES), BF16),
        ),
        in_specs=[VSPEC] * 2,
        out_specs=(VSPEC, VSPEC),
        scratch_shapes=[pltpu.VMEM((MID, 16, 2 * LANES), BF16)],
        compiler_params=PARAMS,
        name="inner",
    )(*in_vmem(done, matrix))


def outer_kernel(own, up, down, matrix, part, done, above, below, lines, high, low):
    zero = jnp.zeros((HALF, 16, 2 * LANES), BF16)
    here = lax.axis_index("row")
    last = lax.axis_size("row") - 1
    place_rows(high, 0, jnp.where(here > 0, above[...].astype(F32), 0.0))
    high[HALF:] = zero
    low[0:HALF] = zero
    place_rows(low, HALF, jnp.where(here < last, below[...].astype(F32), 0.0))
    lines[0:EXT] = done[...]

    def edge(buffer, shift, taps):
        acc = None
        for a in taps:
            layer = buffer[a - shift : a - shift + HALF].reshape(HALF * 16, 2 * LANES)
            term = jnp.dot(layer, matrix[a], preferred_element_type=F32)
            acc = term if acc is None else acc + term
        return acc.reshape(HALF, 16, 2 * LANES)

    top = part[0:HALF] + edge(high, 0, range(HALF))
    bottom = part[HALF:EXT] + edge(low, HALF, range(HALF + 1, FILT))
    for x, q in enumerate(pick((top, bottom), own, up, down, 1)):
        lines[EXT + x] = q.astype(BF16)


def outer_step(own, up, down, matrix, part, done, above, below):
    return pl.pallas_call(
        outer_kernel,
        out_shape=pltpu.VMEM((LINES, 16, LANES), BF16),
        in_specs=[VSPEC] * 8,
        out_specs=VSPEC,
        scratch_shapes=[pltpu.VMEM((EXT, 16, 2 * LANES), BF16)] * 2,
        compiler_params=PARAMS,
        name="outer",
    )(*in_vmem(own, up, down, matrix, part, done, above, below))


def shift_table():
    k = np.arange(2 * LANES)[:, None]
    n = np.arange(NOFF * LANES)[None, :]
    group, c, j = k // LANES, k % LANES // BLK, k % BLK
    want = n % BLK + 2 * (n // LANES - NOFF // 2)
    same = (n % LANES // BLK == c) & (want % BLK == j)
    inside = (want >= 0) & (want < BLK)
    sign = np.where(c == 0, 1.0, -1.0)
    return (same & (inside == (group == 0))) * sign


def gather_kernel(lags, fields, table, out, src, rec, raw):
    lane = lane_ids((NB, LANES))
    j = lane % BLK
    nfreq = fields.shape[0] // SHARE
    for n in range(fields.shape[0]):
        f, m = divmod(n, SHARE)
        line = fields[n].astype(F32)
        src[m, NB * f : NB * f + NB, :] = line[0:NB]
        r = line[NB : 2 * NB]
        sides = jnp.where(j < BLK // 2, next_block(r), prev_block(r))
        rec[m, NB * f : NB * f + NB, 0:LANES] = r.astype(BF16)
        rec[m, NB * f : NB * f + NB, LANES : 2 * LANES] = sides.astype(BF16)
    for i in range(0, NOFF, 2):
        sums = [[], []]
        for m in range(SHARE):
            moved = jnp.dot(
                rec[m], table[:, LANES * i : LANES * i + 2 * LANES], preferred_element_type=F32
            )
            for e in range(2):
                h = i + e - NOFF // 2
                term = (moved[:, LANES * e : LANES * e + LANES] * src[m]).reshape(nfreq, NB, LANES)
                total = jnp.sum(term, axis=0)
                total = total + swap_halves(total)
                sums[e].append(ahead(total, next_block(total), prev_block(total), -h))
        for e in range(2):
            raw[i + e, 0] = jnp.where(lane < BLK, sums[e][0], sums[e][1])
            raw[i + e, 1] = sums[e][2]
    for k in range(NOFF):
        out[2 * k : 2 * k + 2] = raw[lags[k]]


def gather_lags(lags, fields):
    nfreq = fields.shape[0] // SHARE
    table = jnp.asarray(shift_table(), BF16)
    return pl.pallas_call(
        gather_kernel,
        out_shape=pltpu.VMEM((2 * NOFF, NB, LANES), F32),
        in_specs=[SSPEC, VSPEC, VSPEC],
        out_specs=VSPEC,
        scratch_shapes=[
            pltpu.VMEM((SHARE, NB * nfreq, LANES), F32),
            pltpu.VMEM((SHARE, NB * nfreq, 2 * LANES), BF16),
            pltpu.VMEM((NOFF, 2, NB, LANES), F32),
        ],
        compiler_params=PARAMS,
        name="lags",
    )(lags, *in_vmem(fields, table))


def image_kernel(splats, raw, out, rows, nxt, prv, image, sems):
    lane = lane_ids((NB, LANES))

    def piece(depth, x, high):
        line = depth * EXT + x
        s, m = divmod(line, SHARE)
        got = raw[2 * s + m // 2]
        if m == 2 or (m == 1) == high:
            return got
        return swap_halves(got)

    for x in range(EXT):
        v = jnp.where(lane < BLK, piece(0, x, False), piece(1, x, True))
        rows[x] = v
        flipped = swap_halves(v)
        nxt[x] = next_block(flipped)
        prv[x] = prev_block(flipped)
    copies = []
    for group in range(ROWS // 8):
        accs = [None] * 8
        for b in range(OFILT):
            moved = [
                ahead(rows[8 * group + x], nxt[8 * group + x], prv[8 * group + x], b - OHALF)
                for x in range(8 + 2 * OHALF)
            ]
            for a in range(OFILT):
                w = splats[OFILT * a + b]
                for x in range(8):
                    term = moved[x + a] * w
                    accs[x] = term if accs[x] is None else accs[x] + term
        z = jnp.swapaxes(jnp.stack(accs), 0, 1)
        for g in range(WIDTH // LANES):
            even, odd = z[2 * g], z[2 * g + 1]
            cols = slice(LANES * g, LANES * g + LANES)
            image[group, 0, 0, :, cols] = jnp.where(lane < BLK, even, swap_halves(odd))
            image[group, 1, 0, :, cols] = jnp.where(lane < BLK, swap_halves(even), odd)

        copy = pltpu.make_async_copy(
            image.at[group], out.at[:, :, pl.ds(8 * group, 8), :], sems.at[group]
        )
        copy.start()
        copies.append(copy)
    for copy in copies:
        copy.wait()


def filter_image(splats, raw):
    return pl.pallas_call(
        image_kernel,
        out_shape=jax.ShapeDtypeStruct((DEPTHS, 1, ROWS, WIDTH), F32),
        in_specs=[VSPEC, VSPEC],
        out_specs=HBM,
        scratch_shapes=[pltpu.VMEM((EXT, NB, LANES), F32)] * 3
        + [
            pltpu.VMEM((ROWS // 8, DEPTHS, 1, 8, WIDTH), F32),
            pltpu.SemaphoreType.DMA((ROWS // 8,)),
        ],
        compiler_params=PARAMS,
        name="image",
    )(*in_vmem(splats, raw))


def body(source, receiver, filters, table_index, lags, offset_filters):
    count = lax.axis_size("row")

    def shifted(x, step):
        return lax.ppermute(x, "row", [(i, (i + step) % count) for i in range(count)])

    own, south, north, filters, taps = prep(
        source,
        receiver,
        table_index,
        jnp.transpose(filters, (0, 1, 3, 2, 4)),
        jnp.transpose(offset_filters, (1, 0, 2)),
    )
    up = shifted(south, 1)
    down = shifted(north, -1)
    matrix, splats = filter_matrix(filters, taps)
    done, south, north = first_step(own, up, down, matrix)
    above = shifted(south, 1)
    below = shifted(north, -1)
    part, done = inner_step(done, matrix)
    lines = outer_step(own, up, down, matrix, part, done, above, below)
    fields = lax.all_to_all(lines, "freq", 0, 0, tiled=True)
    raw = gather_lags(lags, fields)
    raw = lax.all_to_all(raw, "freq", 0, 0, tiled=True)
    return filter_image(splats, raw)


def solution(mesh):
    in_specs = (
        P("freq", None, "row", None),
        P("freq", None, "row", None),
        P("freq", None, None, None, None),
        P(None, "row", None),
        P(),
        P("freq", None, None),
    )
    out_specs = P(None, "freq", "row", None)
    return jax.shard_map(body, mesh=mesh, in_specs=in_specs, out_specs=out_specs, check_vma=False)
```

```python
import jax
import jax.numpy as jnp
import numpy as np
from jax import lax
from jax.experimental import pallas as pl
from jax.experimental.pallas import tpu as pltpu
from jax.sharding import PartitionSpec as P

NV = 2
FILT = 25
HALF = 12
NOFF = 16
OFILT = 9
OHALF = 4
DEPTHS = 2
ROWS = 16
WIDTH = 512
BLK = 64
NB = 8
LANES = 128
EXT = ROWS + 2 * OHALF
MID = EXT + 2 * HALF
LINES = DEPTHS * EXT
SHARE = LINES // NOFF
F32 = jnp.float32
BF16 = jnp.bfloat16


def lane_ids(shape):
    return lax.broadcasted_iota(jnp.int32, shape, len(shape) - 1)


def block_ids(shape):
    return lax.broadcasted_iota(jnp.int32, shape, len(shape) - 2)


def next_block(x):
    rolled = pltpu.roll(x, NB - 1, x.ndim - 2)
    return jnp.where(block_ids(x.shape) == NB - 1, 0.0, rolled)


def prev_block(x):
    rolled = pltpu.roll(x, 1, x.ndim - 2)
    return jnp.where(block_ids(x.shape) == 0, 0.0, rolled)


def swap_halves(x):
    return pltpu.roll(x, BLK, x.ndim - 1)


def ahead(x, nxt, prv, t):
    if t == 0:
        return x
    j = lane_ids(x.shape) % BLK
    if t > 0:
        return pltpu.roll(jnp.where(j < t, nxt, x), LANES - t, x.ndim - 1)
    return pltpu.roll(jnp.where(j >= BLK + t, prv, x), -t, x.ndim - 1)


def prep_kernel(
    source_in, receiver_in, index_in, filters_in, taps_in,
    own, south, north, filters, taps,
    source, receiver, index, sems,
):
    copies = [
        pltpu.make_async_copy(one, two, sems.at[i])
        for i, (one, two) in enumerate(
            (
                (source_in, source),
                (receiver_in, receiver),
                (index_in, index),
                (filters_in, filters),
                (taps_in, taps),
            )
        )
    ]
    for copy in copies:
        copy.start()
    lane = lane_ids((8, LANES))
    for p in range(3):
        copies[p].wait()
        if p == 0:
            one, two = source[0, 0].astype(F32), source[0, 1].astype(F32)
        elif p == 1:
            one, two = receiver[0, 0].astype(F32), -receiver[0, 1].astype(F32)
        else:
            one, two = index[0].astype(F32), index[1].astype(F32)
        classes = []
        for group in range(ROWS // 8):
            rows = slice(8 * group, 8 * group + 8)
            blocks = []
            for g in range(WIDTH // LANES):
                u = one[rows, LANES * g : LANES * g + LANES]
                v = two[rows, LANES * g : LANES * g + LANES]
                blocks.append(jnp.where(lane < BLK, u, swap_halves(v)))
                blocks.append(jnp.where(lane < BLK, swap_halves(u), v))
            turned = jnp.swapaxes(jnp.stack(blocks), 0, 1)
            subs = slice(8 * p, 8 * p + 8)
            own[rows, subs, :] = turned.astype(BF16)
            if p < 2:
                south[rows, subs, :] = turned.astype(BF16)
                north[rows, subs, :] = turned.astype(BF16)
            classes += [turned[i] for i in range(8)]
        if p == 2:
            for i in range(OHALF):
                at = (ROWS + i // 2, slice(8 * (i % 2), 8 * (i % 2) + 8))
                north[at] = classes[i].astype(BF16)
                south[at] = classes[ROWS - OHALF + i].astype(BF16)
    for copy in copies[3:]:
        copy.wait()


def in_vmem(*arrays):
    return [pltpu.with_memory_space_constraint(x, pltpu.VMEM) for x in arrays]


PARAMS = pltpu.CompilerParams(vmem_limit_bytes=12 << 20)
VSPEC = pl.BlockSpec(memory_space=pltpu.VMEM)
SSPEC = pl.BlockSpec(memory_space=pltpu.SMEM)


HBM = pl.BlockSpec(memory_space=pltpu.HBM)


def prep(*args):
    source, receiver, index, filters, taps = args
    send = pltpu.VMEM((ROWS + 2, 16, LANES), BF16)
    return pl.pallas_call(
        prep_kernel,
        out_shape=(
            pltpu.VMEM((ROWS, 24, LANES), BF16),
            send,
            send,
            pltpu.VMEM(filters.shape, BF16),
            pltpu.VMEM(taps.shape, F32),
        ),
        in_specs=[HBM] * 5,
        out_specs=(VSPEC,) * 5,
        scratch_shapes=[
            pltpu.VMEM(source.shape, BF16),
            pltpu.VMEM(receiver.shape, BF16),
            pltpu.VMEM(index.shape, jnp.int32),
            pltpu.SemaphoreType.DMA((5,)),
        ],
        compiler_params=PARAMS,
        name="prep",
    )(*[pltpu.with_memory_space_constraint(x, pltpu.HBM) for x in args])


def matrix_kernel(filters, taps, out, splats, flat, base):
    tap = lax.broadcasted_iota(jnp.int32, (FILT, LANES), 0)
    col = lane_ids((FILT, LANES)) % BLK
    perm = ((HALF - tap) % BLK == col).astype(BF16)
    for v in range(NV):
        for a in range(FILT):
            flat[v, 2 * a : 2 * a + 2, 0:FILT] = filters[0, v, a].astype(F32)
        base[v] = jnp.dot(
            flat[v, 0 : 2 * FILT, 0:FILT].astype(BF16), perm, preferred_element_type=F32
        )
    lane = lane_ids((16, LANES))
    row = lax.broadcasted_iota(jnp.int32, (16, LANES), 0)
    zero = jnp.zeros((16, LANES), BF16)

    def one_tap(a):
        for v in range(NV):
            turned = []
            for part in range(2):
                taps = jnp.broadcast_to(base[v, 2 * a + part : 2 * a + part + 1, :], (BLK, LANES))
                turned.append(pltpu.roll(taps, 0, 1, stride=1, stride_axis=0))
            cols = slice(v * LANES, v * LANES + LANES)
            for top in range(0, BLK, 16):
                real, imag = (x[top : top + 16] for x in turned)
                near = jnp.abs(row + top - lane % BLK) < BLK // 2
                for c in range(2):
                    if c == 0:
                        band = jnp.where(lane < BLK, real, imag)
                    else:
                        band = jnp.where(lane < BLK, -imag, real)
                    at = c * BLK + top
                    if top in (0, BLK - 16):
                        out[a, at : at + 16, cols] = jnp.where(near, band, 0.0).astype(BF16)
                        at += LANES
                        out[a, at : at + 16, cols] = jnp.where(near, 0.0, band).astype(BF16)
                    else:
                        out[a, at : at + 16, cols] = band.astype(BF16)
                        at += LANES
                        out[a, at : at + 16, cols] = zero

    for a in range(FILT):
        one_tap(a)
    for a in range(OFILT):
        for b in range(OFILT):
            splats[OFILT * a + b] = jnp.broadcast_to(taps[a, 0:1, b : b + 1], (NB, LANES))


def filter_matrix(filters, taps):
    return pl.pallas_call(
        matrix_kernel,
        out_shape=(
            pltpu.VMEM((FILT, 2 * LANES, 2 * LANES), BF16),
            pltpu.VMEM((OFILT * OFILT, NB, LANES), F32),
        ),
        out_specs=(VSPEC, VSPEC),
        scratch_shapes=[
            pltpu.VMEM((NV, 56, LANES), F32),
            pltpu.VMEM((NV, 2 * FILT, LANES), F32),
        ],
        compiler_params=PARAMS,
        name="matrix",
    )(*in_vmem(filters, taps))


def place_rows(buffer, start, rows):
    n = rows.shape[0]
    j = lane_ids((n, NB, LANES)) % BLK
    for f in range(2):
        subs = slice(NB * f, NB * f + NB)
        x = rows[:, subs]
        sides = jnp.where(j < BLK // 2, next_block(x), prev_block(x))
        buffer[start : start + n, subs, 0:LANES] = x.astype(BF16)
        buffer[start : start + n, subs, LANES : 2 * LANES] = sides.astype(BF16)


def filter_rows(buffer, matrix):
    acc = None
    for a in range(FILT):
        layer = buffer[a : a + EXT].reshape(EXT * 16, 2 * LANES)
        term = jnp.dot(layer, matrix[a], preferred_element_type=F32)
        acc = term if acc is None else acc + term
    return acc.reshape(EXT, 16, 2 * LANES)


def pick(acc, own, up, down, depth):
    here = lax.axis_index("row")
    last = lax.axis_size("row") - 1
    lane = lane_ids((NB, LANES))
    rows = []
    for x in range(EXT):
        i = x - OHALF
        if 0 <= i < ROWS:
            both = own[i, 16:24, :].astype(F32)
        else:
            pack, i = (up, x) if x < OHALF else (down, i - ROWS)
            both = pack[ROWS + i // 2, 8 * (i % 2) : 8 * (i % 2) + 8, :].astype(F32)
        swapped = swap_halves(both)
        if depth == 0:
            mask = jnp.where(lane < BLK, both, swapped)
        else:
            mask = jnp.where(lane < BLK, swapped, both)
        mask = jnp.concatenate([mask, mask], axis=0)
        both = acc[x // HALF][x % HALF]
        q = jnp.where(mask == 0.0, both[:, :LANES], both[:, LANES:])
        if x < OHALF:
            q = jnp.where(here > 0, q, 0.0)
        if x >= OHALF + ROWS:
            q = jnp.where(here < last, q, 0.0)
        rows.append(q)
    return rows


def place_sides(buffer, up, down, n, middle):
    here = lax.axis_index("row")
    last = lax.axis_size("row") - 1
    place_rows(buffer, 0, jnp.where(here > 0, up[0:n].astype(F32), 0.0))
    place_rows(buffer, n + middle, jnp.where(here < last, down[0:n].astype(F32), 0.0))


def first_kernel(own, up, down, matrix, lines, south, north, top):
    place_rows(top, ROWS, own[:, 0:16, :].astype(F32))
    place_sides(top, up, down, ROWS, ROWS)
    acc = filter_rows(top, matrix)
    rows = pick((acc[0:HALF], acc[HALF:EXT]), own, up, down, 0)
    for x, q in enumerate(rows):
        lines[x] = q.astype(BF16)
    for i in range(HALF):
        south[i] = rows[OHALF + i].astype(BF16)
        north[i] = rows[2 * OHALF + i].astype(BF16)


def first_step(own, up, down, matrix):
    send = pltpu.VMEM((HALF, 16, LANES), BF16)
    return pl.pallas_call(
        first_kernel,
        out_shape=(pltpu.VMEM((EXT, 16, LANES), BF16), send, send),
        in_specs=[VSPEC] * 4,
        out_specs=(VSPEC,) * 3,
        scratch_shapes=[pltpu.VMEM((MID, 16, 2 * LANES), BF16)],
        compiler_params=PARAMS,
        name="first",
    )(*in_vmem(own, up, down, matrix))


def inner_kernel(done, matrix, acc, lines, mid):
    zero = jnp.zeros((HALF, 16, 2 * LANES), BF16)
    mid[0:HALF] = zero
    mid[HALF + EXT :] = zero
    place_rows(mid, HALF, done[...].astype(F32))
    acc[...] = filter_rows(mid, matrix)
    lines[...] = done[...]


def inner_step(done, matrix):
    return pl.pallas_call(
        inner_kernel,
        out_shape=(
            pltpu.VMEM((EXT, 16, 2 * LANES), F32),
            pltpu.VMEM((EXT, 16, LANES), BF16),
        ),
        in_specs=[VSPEC] * 2,
        out_specs=(VSPEC, VSPEC),
        scratch_shapes=[pltpu.VMEM((MID, 16, 2 * LANES), BF16)],
        compiler_params=PARAMS,
        name="inner",
    )(*in_vmem(done, matrix))


def outer_kernel(own, up, down, matrix, part, done, above, below, lines, high, low):
    zero = jnp.zeros((HALF, 16, 2 * LANES), BF16)
    here = lax.axis_index("row")
    last = lax.axis_size("row") - 1
    place_rows(high, 0, jnp.where(here > 0, above[...].astype(F32), 0.0))
    high[HALF:] = zero
    low[0:HALF] = zero
    place_rows(low, HALF, jnp.where(here < last, below[...].astype(F32), 0.0))
    lines[0:EXT] = done[...]

    def edge(buffer, start, count, taps):
        acc = None
        for a in taps:
            at = start + a
            layer = buffer[at : at + count].reshape(count * 16, 2 * LANES)
            term = jnp.dot(layer, matrix[a], preferred_element_type=F32)
            acc = term if acc is None else acc + term
        return acc.reshape(count, 16, 2 * LANES)

    few = HALF // 2
    wide = part[0:HALF] + edge(high, 0, HALF, range(few))
    top = jnp.concatenate([wide[:few] + edge(high, 0, few, range(few, HALF)), wide[few:]], axis=0)
    wide = part[HALF:EXT] + edge(low, -HALF, HALF, range(HALF + 1 + few, FILT))
    rest = edge(low, few - HALF, few, range(HALF + 1, HALF + 1 + few))
    bottom = jnp.concatenate([wide[:few], wide[few:] + rest], axis=0)
    for x, q in enumerate(pick((top, bottom), own, up, down, 1)):
        lines[EXT + x] = q.astype(BF16)


def outer_step(own, up, down, matrix, part, done, above, below):
    return pl.pallas_call(
        outer_kernel,
        out_shape=pltpu.VMEM((LINES, 16, LANES), BF16),
        in_specs=[VSPEC] * 8,
        out_specs=VSPEC,
        scratch_shapes=[pltpu.VMEM((EXT, 16, 2 * LANES), BF16)] * 2,
        compiler_params=PARAMS,
        name="outer",
    )(*in_vmem(own, up, down, matrix, part, done, above, below))


def shift_table():
    k = np.arange(2 * LANES)[:, None]
    n = np.arange(NOFF * LANES)[None, :]
    group, c, j = k // LANES, k % LANES // BLK, k % BLK
    want = n % BLK + 2 * (n // LANES - NOFF // 2)
    same = (n % LANES // BLK == c) & (want % BLK == j)
    inside = (want >= 0) & (want < BLK)
    sign = np.where(c == 0, 1.0, -1.0)
    return (same & (inside == (group == 0))) * sign


def gather_kernel(lags, fields, table, out, src, rec, raw):
    lane = lane_ids((NB, LANES))
    j = lane % BLK
    nfreq = fields.shape[0] // SHARE
    for n in range(fields.shape[0]):
        f, m = divmod(n, SHARE)
        line = fields[n].astype(F32)
        src[m, NB * f : NB * f + NB, :] = line[0:NB]
        r = line[NB : 2 * NB]
        sides = jnp.where(j < BLK // 2, next_block(r), prev_block(r))
        rec[m, NB * f : NB * f + NB, 0:LANES] = r.astype(BF16)
        rec[m, NB * f : NB * f + NB, LANES : 2 * LANES] = sides.astype(BF16)
    for i in range(0, NOFF, 2):
        sums = [[], []]
        for m in range(SHARE):
            moved = jnp.dot(
                rec[m], table[:, LANES * i : LANES * i + 2 * LANES], preferred_element_type=F32
            )
            for e in range(2):
                h = i + e - NOFF // 2
                term = (moved[:, LANES * e : LANES * e + LANES] * src[m]).reshape(nfreq, NB, LANES)
                total = jnp.sum(term, axis=0)
                total = total + swap_halves(total)
                sums[e].append(ahead(total, next_block(total), prev_block(total), -h))
        for e in range(2):
            raw[i + e, 0] = jnp.where(lane < BLK, sums[e][0], sums[e][1])
            raw[i + e, 1] = sums[e][2]
    for k in range(NOFF):
        out[2 * k : 2 * k + 2] = raw[lags[k]]


def gather_lags(lags, fields):
    nfreq = fields.shape[0] // SHARE
    table = jnp.asarray(shift_table(), BF16)
    return pl.pallas_call(
        gather_kernel,
        out_shape=pltpu.VMEM((2 * NOFF, NB, LANES), F32),
        in_specs=[SSPEC, VSPEC, VSPEC],
        out_specs=VSPEC,
        scratch_shapes=[
            pltpu.VMEM((SHARE, NB * nfreq, LANES), F32),
            pltpu.VMEM((SHARE, NB * nfreq, 2 * LANES), BF16),
            pltpu.VMEM((NOFF, 2, NB, LANES), F32),
        ],
        compiler_params=PARAMS,
        name="lags",
    )(lags, *in_vmem(fields, table))


def image_kernel(splats, raw, out, rows, nxt, prv, image, sems):
    lane = lane_ids((NB, LANES))

    def piece(depth, x, high):
        line = depth * EXT + x
        s, m = divmod(line, SHARE)
        got = raw[2 * s + m // 2]
        if m == 2 or (m == 1) == high:
            return got
        return swap_halves(got)

    for x in range(EXT):
        v = jnp.where(lane < BLK, piece(0, x, False), piece(1, x, True))
        rows[x] = v
        flipped = swap_halves(v)
        nxt[x] = next_block(flipped)
        prv[x] = prev_block(flipped)
    copies = []
    for group in range(ROWS // 8):
        accs = [None] * 8
        for b in range(OFILT):
            moved = [
                ahead(rows[8 * group + x], nxt[8 * group + x], prv[8 * group + x], b - OHALF)
                for x in range(8 + 2 * OHALF)
            ]
            for a in range(OFILT):
                w = splats[OFILT * a + b]
                for x in range(8):
                    term = moved[x + a] * w
                    accs[x] = term if accs[x] is None else accs[x] + term
        z = jnp.swapaxes(jnp.stack(accs), 0, 1)
        for g in range(WIDTH // LANES):
            even, odd = z[2 * g], z[2 * g + 1]
            cols = slice(LANES * g, LANES * g + LANES)
            image[group, 0, 0, :, cols] = jnp.where(lane < BLK, even, swap_halves(odd))
            image[group, 1, 0, :, cols] = jnp.where(lane < BLK, swap_halves(even), odd)

        copy = pltpu.make_async_copy(
            image.at[group], out.at[:, :, pl.ds(8 * group, 8), :], sems.at[group]
        )
        copy.start()
        copies.append(copy)
    for copy in copies:
        copy.wait()


def filter_image(splats, raw):
    return pl.pallas_call(
        image_kernel,
        out_shape=jax.ShapeDtypeStruct((DEPTHS, 1, ROWS, WIDTH), F32),
        in_specs=[VSPEC, VSPEC],
        out_specs=HBM,
        scratch_shapes=[pltpu.VMEM((EXT, NB, LANES), F32)] * 3
        + [
            pltpu.VMEM((ROWS // 8, DEPTHS, 1, 8, WIDTH), F32),
            pltpu.SemaphoreType.DMA((ROWS // 8,)),
        ],
        compiler_params=PARAMS,
        name="image",
    )(*in_vmem(splats, raw))


def body(source, receiver, filters, table_index, lags, offset_filters):
    count = lax.axis_size("row")

    def shifted(x, step):
        return lax.ppermute(x, "row", [(i, (i + step) % count) for i in range(count)])

    own, south, north, filters, taps = prep(
        source,
        receiver,
        table_index,
        jnp.transpose(filters, (0, 1, 3, 2, 4)),
        jnp.transpose(offset_filters, (1, 0, 2)),
    )
    up = shifted(south, 1)
    down = shifted(north, -1)
    matrix, splats = filter_matrix(filters, taps)
    done, south, north = first_step(own, up, down, matrix)
    above = shifted(south, 1)
    below = shifted(north, -1)
    part, done = inner_step(done, matrix)
    lines = outer_step(own, up, down, matrix, part, done, above, below)
    fields = lax.all_to_all(lines, "freq", 0, 0, tiled=True)
    raw = gather_lags(lags, fields)
    raw = lax.all_to_all(raw, "freq", 0, 0, tiled=True)
    return filter_image(splats, raw)


def solution(mesh):
    in_specs = (
        P("freq", None, "row", None),
        P("freq", None, "row", None),
        P("freq", None, None, None, None),
        P(None, "row", None),
        P(),
        P("freq", None, None),
    )
    out_specs = P(None, "freq", "row", None)
    return jax.shard_map(body, mesh=mesh, in_specs=in_specs, out_specs=out_specs, check_vma=False)
```

```python
import jax
import jax.numpy as jnp
import numpy as np
from jax import lax
from jax.experimental import pallas as pl
from jax.experimental.pallas import tpu as pltpu
from jax.sharding import PartitionSpec as P

NV = 2
FILT = 25
HALF = 12
NOFF = 16
OFILT = 9
OHALF = 4
DEPTHS = 2
ROWS = 16
WIDTH = 512
BLK = 64
NB = 8
LANES = 128
EXT = ROWS + 2 * OHALF
MID = EXT + 2 * HALF
LINES = DEPTHS * EXT
SHARE = LINES // NOFF
F32 = jnp.float32
BF16 = jnp.bfloat16


def lane_ids(shape):
    return lax.broadcasted_iota(jnp.int32, shape, len(shape) - 1)


def block_ids(shape):
    return lax.broadcasted_iota(jnp.int32, shape, len(shape) - 2)


def next_block(x):
    rolled = pltpu.roll(x, NB - 1, x.ndim - 2)
    return jnp.where(block_ids(x.shape) == NB - 1, 0.0, rolled)


def prev_block(x):
    rolled = pltpu.roll(x, 1, x.ndim - 2)
    return jnp.where(block_ids(x.shape) == 0, 0.0, rolled)


def swap_halves(x):
    return pltpu.roll(x, BLK, x.ndim - 1)


def ahead(x, nxt, prv, t):
    if t == 0:
        return x
    j = lane_ids(x.shape) % BLK
    if t > 0:
        return pltpu.roll(jnp.where(j < t, nxt, x), LANES - t, x.ndim - 1)
    return pltpu.roll(jnp.where(j >= BLK + t, prv, x), -t, x.ndim - 1)


def prep_kernel(
    source_in, receiver_in, index_in, filters_in, taps_in,
    own, south, north, filters, taps,
    source, receiver, index, sems,
):
    copies = [
        pltpu.make_async_copy(one, two, sems.at[i])
        for i, (one, two) in enumerate(
            (
                (source_in, source),
                (receiver_in, receiver),
                (index_in, index),
                (filters_in, filters),
                (taps_in, taps),
            )
        )
    ]
    for copy in copies:
        copy.start()
    lane = lane_ids((8, LANES))
    for p in range(3):
        copies[p].wait()
        if p == 0:
            one, two = source[0, 0].astype(F32), source[0, 1].astype(F32)
        elif p == 1:
            one, two = receiver[0, 0].astype(F32), -receiver[0, 1].astype(F32)
        else:
            one, two = index[0].astype(F32), index[1].astype(F32)
        classes = []
        for group in range(ROWS // 8):
            rows = slice(8 * group, 8 * group + 8)
            blocks = []
            for g in range(WIDTH // LANES):
                u = one[rows, LANES * g : LANES * g + LANES]
                v = two[rows, LANES * g : LANES * g + LANES]
                blocks.append(jnp.where(lane < BLK, u, swap_halves(v)))
                blocks.append(jnp.where(lane < BLK, swap_halves(u), v))
            turned = jnp.swapaxes(jnp.stack(blocks), 0, 1)
            subs = slice(8 * p, 8 * p + 8)
            own[rows, subs, :] = turned.astype(BF16)
            if p < 2:
                south[rows, subs, :] = turned.astype(BF16)
                north[rows, subs, :] = turned.astype(BF16)
            classes += [turned[i] for i in range(8)]
        if p == 2:
            for i in range(OHALF):
                at = (ROWS + i // 2, slice(8 * (i % 2), 8 * (i % 2) + 8))
                north[at] = classes[i].astype(BF16)
                south[at] = classes[ROWS - OHALF + i].astype(BF16)
    for copy in copies[3:]:
        copy.wait()


def in_vmem(*arrays):
    return [pltpu.with_memory_space_constraint(x, pltpu.VMEM) for x in arrays]


PARAMS = pltpu.CompilerParams(vmem_limit_bytes=12 << 20)
VSPEC = pl.BlockSpec(memory_space=pltpu.VMEM)
SSPEC = pl.BlockSpec(memory_space=pltpu.SMEM)


HBM = pl.BlockSpec(memory_space=pltpu.HBM)


def prep(*args):
    source, receiver, index, filters, taps = args
    send = pltpu.VMEM((ROWS + 2, 16, LANES), BF16)
    return pl.pallas_call(
        prep_kernel,
        out_shape=(
            pltpu.VMEM((ROWS, 24, LANES), BF16),
            send,
            send,
            pltpu.VMEM(filters.shape, BF16),
            pltpu.VMEM(taps.shape, F32),
        ),
        in_specs=[HBM] * 5,
        out_specs=(VSPEC,) * 5,
        scratch_shapes=[
            pltpu.VMEM(source.shape, BF16),
            pltpu.VMEM(receiver.shape, BF16),
            pltpu.VMEM(index.shape, jnp.int32),
            pltpu.SemaphoreType.DMA((5,)),
        ],
        compiler_params=PARAMS,
        name="prep",
    )(*[pltpu.with_memory_space_constraint(x, pltpu.HBM) for x in args])


def matrix_kernel(filters, taps, out, splats, flat, base):
    tap = lax.broadcasted_iota(jnp.int32, (FILT, LANES), 0)
    col = lane_ids((FILT, LANES)) % BLK
    perm = ((HALF - tap) % BLK == col).astype(BF16)
    for v in range(NV):
        for a in range(FILT):
            flat[v, 2 * a : 2 * a + 2, 0:FILT] = filters[0, v, a].astype(F32)
        base[v] = jnp.dot(
            flat[v, 0 : 2 * FILT, 0:FILT].astype(BF16), perm, preferred_element_type=F32
        )
    lane = lane_ids((16, LANES))
    row = lax.broadcasted_iota(jnp.int32, (16, LANES), 0)
    zero = jnp.zeros((16, LANES), BF16)

    def one_tap(a):
        for v in range(NV):
            turned = []
            for part in range(2):
                taps = jnp.broadcast_to(base[v, 2 * a + part : 2 * a + part + 1, :], (BLK, LANES))
                turned.append(pltpu.roll(taps, 0, 1, stride=1, stride_axis=0))
            cols = slice(v * LANES, v * LANES + LANES)
            for top in range(0, BLK, 16):
                real, imag = (x[top : top + 16] for x in turned)
                near = jnp.abs(row + top - lane % BLK) < BLK // 2
                for c in range(2):
                    if c == 0:
                        band = jnp.where(lane < BLK, real, imag)
                    else:
                        band = jnp.where(lane < BLK, -imag, real)
                    at = c * BLK + top
                    if top in (0, BLK - 16):
                        out[a, at : at + 16, cols] = jnp.where(near, band, 0.0).astype(BF16)
                        at += LANES
                        out[a, at : at + 16, cols] = jnp.where(near, 0.0, band).astype(BF16)
                    else:
                        out[a, at : at + 16, cols] = band.astype(BF16)
                        at += LANES
                        out[a, at : at + 16, cols] = zero

    for a in range(FILT):
        one_tap(a)
    for a in range(OFILT):
        for b in range(OFILT):
            splats[OFILT * a + b] = jnp.broadcast_to(taps[a, 0:1, b : b + 1], (NB, LANES))


def filter_matrix(filters, taps):
    return pl.pallas_call(
        matrix_kernel,
        out_shape=(
            pltpu.VMEM((FILT, 2 * LANES, 2 * LANES), BF16),
            pltpu.VMEM((OFILT * OFILT, NB, LANES), F32),
        ),
        out_specs=(VSPEC, VSPEC),
        scratch_shapes=[
            pltpu.VMEM((NV, 56, LANES), F32),
            pltpu.VMEM((NV, 2 * FILT, LANES), F32),
        ],
        compiler_params=PARAMS,
        name="matrix",
    )(*in_vmem(filters, taps))


def place_rows(buffer, start, rows):
    n = rows.shape[0]
    j = lane_ids((n, NB, LANES)) % BLK
    for f in range(2):
        subs = slice(NB * f, NB * f + NB)
        x = rows[:, subs]
        sides = jnp.where(j < BLK // 2, next_block(x), prev_block(x))
        buffer[start : start + n, subs, 0:LANES] = x.astype(BF16)
        buffer[start : start + n, subs, LANES : 2 * LANES] = sides.astype(BF16)


def filter_rows(buffer, matrix):
    acc = None
    for a in range(FILT):
        layer = buffer[a : a + EXT].reshape(EXT * 16, 2 * LANES)
        term = jnp.dot(layer, matrix[a], preferred_element_type=F32)
        acc = term if acc is None else acc + term
    return acc.reshape(EXT, 16, 2 * LANES)


def pick(acc, own, up, down, depth):
    here = lax.axis_index("row")
    last = lax.axis_size("row") - 1
    lane = lane_ids((NB, LANES))
    rows = []
    for x in range(EXT):
        i = x - OHALF
        if 0 <= i < ROWS:
            both = own[i, 16:24, :].astype(F32)
        else:
            pack, i = (up, x) if x < OHALF else (down, i - ROWS)
            both = pack[ROWS + i // 2, 8 * (i % 2) : 8 * (i % 2) + 8, :].astype(F32)
        swapped = swap_halves(both)
        if depth == 0:
            mask = jnp.where(lane < BLK, both, swapped)
        else:
            mask = jnp.where(lane < BLK, swapped, both)
        mask = jnp.concatenate([mask, mask], axis=0)
        both = acc[x // HALF][x % HALF]
        q = jnp.where(mask == 0.0, both[:, :LANES], both[:, LANES:])
        if x < OHALF:
            q = jnp.where(here > 0, q, 0.0)
        if x >= OHALF + ROWS:
            q = jnp.where(here < last, q, 0.0)
        rows.append(q)
    return rows


def place_sides(buffer, up, down, n, middle):
    here = lax.axis_index("row")
    last = lax.axis_size("row") - 1
    place_rows(buffer, 0, jnp.where(here > 0, up[0:n].astype(F32), 0.0))
    place_rows(buffer, n + middle, jnp.where(here < last, down[0:n].astype(F32), 0.0))


def first_kernel(own, up, down, matrix, lines, south, north, top):
    place_rows(top, ROWS, own[:, 0:16, :].astype(F32))
    place_sides(top, up, down, ROWS, ROWS)
    acc = filter_rows(top, matrix)
    rows = pick((acc[0:HALF], acc[HALF:EXT]), own, up, down, 0)
    for x, q in enumerate(rows):
        lines[x] = q.astype(BF16)
    for i in range(HALF):
        south[i] = rows[OHALF + i].astype(BF16)
        north[i] = rows[2 * OHALF + i].astype(BF16)


def first_step(own, up, down, matrix):
    send = pltpu.VMEM((HALF, 16, LANES), BF16)
    return pl.pallas_call(
        first_kernel,
        out_shape=(pltpu.VMEM((EXT, 16, LANES), BF16), send, send),
        in_specs=[VSPEC] * 4,
        out_specs=(VSPEC,) * 3,
        scratch_shapes=[pltpu.VMEM((MID, 16, 2 * LANES), BF16)],
        compiler_params=PARAMS,
        name="first",
    )(*in_vmem(own, up, down, matrix))


def inner_kernel(done, matrix, acc, mid):
    zero = jnp.zeros((HALF, 16, 2 * LANES), BF16)
    mid[0:HALF] = zero
    mid[HALF + EXT :] = zero
    place_rows(mid, HALF, done[...].astype(F32))
    acc[...] = filter_rows(mid, matrix)


def inner_step(done, matrix):
    return pl.pallas_call(
        inner_kernel,
        out_shape=pltpu.VMEM((EXT, 16, 2 * LANES), F32),
        in_specs=[VSPEC] * 2,
        out_specs=VSPEC,
        scratch_shapes=[pltpu.VMEM((MID, 16, 2 * LANES), BF16)],
        compiler_params=PARAMS,
        name="inner",
    )(*in_vmem(done, matrix))


def outer_kernel(own, up, down, matrix, part, done, above, below, lines, high, low):
    zero = jnp.zeros((HALF, 16, 2 * LANES), BF16)
    here = lax.axis_index("row")
    last = lax.axis_size("row") - 1
    place_rows(high, 0, jnp.where(here > 0, above[...].astype(F32), 0.0))
    high[HALF:] = zero
    low[0:HALF] = zero
    place_rows(low, HALF, jnp.where(here < last, below[...].astype(F32), 0.0))
    lines[0:EXT] = done[...]

    def edge(buffer, start, count, taps):
        acc = None
        for a in taps:
            at = start + a
            layer = buffer[at : at + count].reshape(count * 16, 2 * LANES)
            term = jnp.dot(layer, matrix[a], preferred_element_type=F32)
            acc = term if acc is None else acc + term
        return acc.reshape(count, 16, 2 * LANES)

    few = HALF // 2
    wide = part[0:HALF] + edge(high, 0, HALF, range(few))
    top = jnp.concatenate([wide[:few] + edge(high, 0, few, range(few, HALF)), wide[few:]], axis=0)
    wide = part[HALF:EXT] + edge(low, -HALF, HALF, range(HALF + 1 + few, FILT))
    rest = edge(low, few - HALF, few, range(HALF + 1, HALF + 1 + few))
    bottom = jnp.concatenate([wide[:few], wide[few:] + rest], axis=0)
    for x, q in enumerate(pick((top, bottom), own, up, down, 1)):
        lines[EXT + x] = q.astype(BF16)


def outer_step(own, up, down, matrix, part, done, above, below):
    return pl.pallas_call(
        outer_kernel,
        out_shape=pltpu.VMEM((LINES, 16, LANES), BF16),
        in_specs=[VSPEC] * 8,
        out_specs=VSPEC,
        scratch_shapes=[pltpu.VMEM((EXT, 16, 2 * LANES), BF16)] * 2,
        compiler_params=PARAMS,
        name="outer",
    )(*in_vmem(own, up, down, matrix, part, done, above, below))


def shift_table():
    k = np.arange(2 * LANES)[:, None]
    n = np.arange(NOFF * LANES)[None, :]
    group, c, j = k // LANES, k % LANES // BLK, k % BLK
    want = n % BLK + 2 * (n // LANES - NOFF // 2)
    same = (n % LANES // BLK == c) & (want % BLK == j)
    inside = (want >= 0) & (want < BLK)
    sign = np.where(c == 0, 1.0, -1.0)
    return (same & (inside == (group == 0))) * sign


def gather_kernel(lags, fields, table, out, src, rec, raw):
    lane = lane_ids((NB, LANES))
    j = lane % BLK
    nfreq = fields.shape[0] // SHARE
    for n in range(fields.shape[0]):
        f, m = divmod(n, SHARE)
        line = fields[n].astype(F32)
        src[m, NB * f : NB * f + NB, :] = line[0:NB]
        r = line[NB : 2 * NB]
        sides = jnp.where(j < BLK // 2, next_block(r), prev_block(r))
        rec[m, NB * f : NB * f + NB, 0:LANES] = r.astype(BF16)
        rec[m, NB * f : NB * f + NB, LANES : 2 * LANES] = sides.astype(BF16)
    for i in range(0, NOFF, 2):
        sums = [[], []]
        for m in range(SHARE):
            moved = jnp.dot(
                rec[m], table[:, LANES * i : LANES * i + 2 * LANES], preferred_element_type=F32
            )
            for e in range(2):
                h = i + e - NOFF // 2
                term = (moved[:, LANES * e : LANES * e + LANES] * src[m]).reshape(nfreq, NB, LANES)
                total = jnp.sum(term, axis=0)
                total = total + swap_halves(total)
                sums[e].append(ahead(total, next_block(total), prev_block(total), -h))
        for e in range(2):
            raw[i + e, 0] = jnp.where(lane < BLK, sums[e][0], sums[e][1])
            raw[i + e, 1] = sums[e][2]
    for k in range(NOFF):
        out[2 * k : 2 * k + 2] = raw[lags[k]]


def gather_lags(lags, fields):
    nfreq = fields.shape[0] // SHARE
    table = jnp.asarray(shift_table(), BF16)
    return pl.pallas_call(
        gather_kernel,
        out_shape=pltpu.VMEM((2 * NOFF, NB, LANES), F32),
        in_specs=[SSPEC, VSPEC, VSPEC],
        out_specs=VSPEC,
        scratch_shapes=[
            pltpu.VMEM((SHARE, NB * nfreq, LANES), F32),
            pltpu.VMEM((SHARE, NB * nfreq, 2 * LANES), BF16),
            pltpu.VMEM((NOFF, 2, NB, LANES), F32),
        ],
        compiler_params=PARAMS,
        name="lags",
    )(lags, *in_vmem(fields, table))


def image_kernel(splats, raw, out, rows, nxt, prv, image, sems):
    lane = lane_ids((NB, LANES))

    def piece(depth, x, high):
        line = depth * EXT + x
        s, m = divmod(line, SHARE)
        got = raw[2 * s + m // 2]
        if m == 2 or (m == 1) == high:
            return got
        return swap_halves(got)

    for x in range(EXT):
        v = jnp.where(lane < BLK, piece(0, x, False), piece(1, x, True))
        rows[x] = v
        flipped = swap_halves(v)
        nxt[x] = next_block(flipped)
        prv[x] = prev_block(flipped)
    copies = []
    for group in range(ROWS // 8):
        accs = [None] * 8
        for b in range(OFILT):
            moved = [
                ahead(rows[8 * group + x], nxt[8 * group + x], prv[8 * group + x], b - OHALF)
                for x in range(8 + 2 * OHALF)
            ]
            for a in range(OFILT):
                w = splats[OFILT * a + b]
                for x in range(8):
                    term = moved[x + a] * w
                    accs[x] = term if accs[x] is None else accs[x] + term
        z = jnp.swapaxes(jnp.stack(accs), 0, 1)
        for g in range(WIDTH // LANES):
            even, odd = z[2 * g], z[2 * g + 1]
            cols = slice(LANES * g, LANES * g + LANES)
            image[group, 0, 0, :, cols] = jnp.where(lane < BLK, even, swap_halves(odd))
            image[group, 1, 0, :, cols] = jnp.where(lane < BLK, swap_halves(even), odd)

        copy = pltpu.make_async_copy(
            image.at[group], out.at[:, :, pl.ds(8 * group, 8), :], sems.at[group]
        )
        copy.start()
        copies.append(copy)
    for copy in copies:
        copy.wait()


def filter_image(splats, raw):
    return pl.pallas_call(
        image_kernel,
        out_shape=jax.ShapeDtypeStruct((DEPTHS, 1, ROWS, WIDTH), F32),
        in_specs=[VSPEC, VSPEC],
        out_specs=HBM,
        scratch_shapes=[pltpu.VMEM((EXT, NB, LANES), F32)] * 3
        + [
            pltpu.VMEM((ROWS // 8, DEPTHS, 1, 8, WIDTH), F32),
            pltpu.SemaphoreType.DMA((ROWS // 8,)),
        ],
        compiler_params=PARAMS,
        name="image",
    )(*in_vmem(splats, raw))


def body(source, receiver, filters, table_index, lags, offset_filters):
    count = lax.axis_size("row")

    def shifted(x, step):
        return lax.ppermute(x, "row", [(i, (i + step) % count) for i in range(count)])

    own, south, north, filters, taps = prep(
        source,
        receiver,
        table_index,
        jnp.transpose(filters, (0, 1, 3, 2, 4)),
        jnp.transpose(offset_filters, (1, 0, 2)),
    )
    up = shifted(south, 1)
    down = shifted(north, -1)
    matrix, splats = filter_matrix(filters, taps)
    done, south, north = first_step(own, up, down, matrix)
    above = shifted(south, 1)
    below = shifted(north, -1)
    part = inner_step(done, matrix)
    lines = outer_step(own, up, down, matrix, part, done, above, below)
    fields = lax.all_to_all(lines, "freq", 0, 0, tiled=True)
    raw = gather_lags(lags, fields)
    raw = lax.all_to_all(raw, "freq", 0, 0, tiled=True)
    return filter_image(splats, raw)


def solution(mesh):
    in_specs = (
        P("freq", None, "row", None),
        P("freq", None, "row", None),
        P("freq", None, None, None, None),
        P(None, "row", None),
        P(),
        P("freq", None, None),
    )
    out_specs = P(None, "freq", "row", None)
    return jax.shard_map(body, mesh=mesh, in_specs=in_specs, out_specs=out_specs, check_vma=False)
```
